32 devices in a mesh: grp: 4 (over x, core), uly: 8 (over z, y).
Axes of the slice: x: 2, y: 2, z: 4, core: 2. Of those that a mesh axis runs over, the one named last changes fastest.
Arguments:
- queries: bfloat16 [4096, 8192], P(('grp', 'uly')), may hold values from -6 to 6
- key_state_rows: bfloat16 [4096, 1024], P(('grp', 'uly')), may hold values from -6 to 6
- value_state_rows: bfloat16 [4096, 1024], P(('grp', 'uly')), may hold values from -6 to 6
- vert_blocks: int32 [64, 6], replicated, may hold values from -1 to 31, as said below
- slash_offsets: int32 [64, 3], replicated, may hold values from -1 to 4, as said below
Outputs:
- attended: bfloat16 [4096, 8192], P(('grp', 'uly'))
The draws below stay inside these ranges and needn't reach their ends.
Inputs may be any that keep to these rules, and one draw needn't show every extreme that they name: `vert_blocks`: row h lists distinct block numbers first and -1 in the slots after them; every row lists one block or more and some row lists 6. `slash_offsets`: row h lists distinct offsets of at least 1 first and -1 in the slots after them; every row lists one offset or more and some row lists 3.
All inputs are finite; a program needn't handle non-finite values.
Results may differ from the reference program's by a relative error of at most 0.005.
Values may be sent and summed in bfloat16 or wider, within the bound.
A program may use at most 128 MiB of HBM per device.

```python
import jax
import jax.numpy as jnp
from jax import lax

QUERY_HEADS = 64
KEY_VALUE_HEADS = 8
HEAD_SIZE = 128
BLOCK_TOKENS = 128
NV = 6
NS = 3
TOTAL_TOKENS = 4096
NBLK = 32
SPAN = 4


def draw_queries(key, part):
    random_jitter = jax.random.normal(jax.random.fold_in(key, 1), (TOTAL_TOKENS, QUERY_HEADS, HEAD_SIZE), dtype=jnp.float32)
    random_jitter = jnp.clip(random_jitter, -6.0, 6.0)
    return random_jitter.reshape(TOTAL_TOKENS, QUERY_HEADS * HEAD_SIZE).astype(jnp.bfloat16)


def draw_key_state_rows(key, part):
    random_jitter = jax.random.normal(jax.random.fold_in(key, 2), (TOTAL_TOKENS, KEY_VALUE_HEADS, HEAD_SIZE), dtype=jnp.float32)
    random_jitter = jnp.clip(random_jitter, -6.0, 6.0)
    return random_jitter.reshape(TOTAL_TOKENS, KEY_VALUE_HEADS * HEAD_SIZE).astype(jnp.bfloat16)


def draw_vert_blocks(key, part):
    head_keys = jax.random.split(jax.random.fold_in(key, 11), QUERY_HEADS)

    def pick_blocks(head_key):
        return jax.random.permutation(head_key, NBLK)[:NV]
    picks = jax.vmap(pick_blocks)(head_keys).astype(jnp.int32)
    heavy = jax.random.randint(jax.random.fold_in(key, 12), (QUERY_HEADS,), 0, 4) == 0
    lighter = jax.random.randint(jax.random.fold_in(key, 13), (QUERY_HEADS,), 1, 3)
    full_head = jax.random.randint(jax.random.fold_in(key, 14), (), 0, QUERY_HEADS)
    counts = jnp.where(heavy | (jnp.arange(QUERY_HEADS) == full_head), NV, lighter)
    return jnp.where(jnp.arange(NV)[None, :] < counts[:, None], picks, -1).astype(jnp.int32)


def draw_slash_offsets(key, part):
    head_keys = jax.random.split(jax.random.fold_in(key, 21), QUERY_HEADS)

    def pick_offsets(head_key):
        return jax.random.permutation(head_key, SPAN)[:NS] + 1
    picks = jax.vmap(pick_offsets)(head_keys).astype(jnp.int32)
    counts = jax.random.randint(jax.random.fold_in(key, 22), (QUERY_HEADS,), 1, NS + 1)
    full_head = jax.random.randint(jax.random.fold_in(key, 23), (), 0, QUERY_HEADS)
    counts = jnp.where(jnp.arange(QUERY_HEADS) == full_head, NS, counts)
    return jnp.where(jnp.arange(NS)[None, :] < counts[:, None], picks, -1).astype(jnp.int32)


def steps_of(stream_key, extent, cuts, low, top_value):
    level = 1.0
    for position, blocks in cuts:
        draws = jax.random.uniform(jax.random.fold_in(jax.random.fold_in(stream_key, 6), position), (blocks,), jnp.float32, low / len(cuts), top_value / len(cuts))
        level = level * jnp.repeat(jnp.exp(draws), extent[position] // blocks).reshape((-1,) + (1,) * (len(extent) - 1 - position))
    return level


def gaussian(key, shape, width, limit, cuts=(), kind=jnp.bfloat16):
    values = width * jax.random.normal(key, shape, jnp.float32)
    if cuts:
        values = values * steps_of(key, shape, cuts, -0.22, 0.18)
    return jnp.clip(values, -limit, limit).astype(kind)


def setup_inputs(seed: int = 0) -> dict:
    streams_of = jax.random.split(jax.random.key(seed), 6)
    return {
        "queries": draw_queries(jax.random.fold_in(streams_of[5], 71), 0),
        "key_state_rows": draw_key_state_rows(jax.random.fold_in(streams_of[5], 71), 0),
        "value_state_rows": gaussian(streams_of[2], (TOTAL_TOKENS, KEY_VALUE_HEADS * HEAD_SIZE), 1.0, 6.0, ((0, 32),)),
        "vert_blocks": draw_vert_blocks(jax.random.fold_in(streams_of[5], 71), 0),
        "slash_offsets": draw_slash_offsets(jax.random.fold_in(streams_of[5], 71), 0),
    }


neg_large = -1.0e30


def reference(queries, key_state_rows, value_state_rows, vert_blocks, slash_offsets):
    group_width = QUERY_HEADS // KEY_VALUE_HEADS
    total_blocks = TOTAL_TOKENS // BLOCK_TOKENS
    score_scale = HEAD_SIZE ** -0.5
    q_tiles = queries.reshape(total_blocks, BLOCK_TOKENS, QUERY_HEADS, HEAD_SIZE)
    key_block_tiles = key_state_rows.reshape(total_blocks, BLOCK_TOKENS, KEY_VALUE_HEADS, HEAD_SIZE)
    value_block_tiles = value_state_rows.reshape(total_blocks, BLOCK_TOKENS, KEY_VALUE_HEADS, HEAD_SIZE)
    blocks = jnp.arange(total_blocks, dtype=jnp.int32)
    causal = jnp.arange(BLOCK_TOKENS)[:, None] >= jnp.arange(BLOCK_TOKENS)[None, :]
    slot_total = 1 + NS + NV
    first_slot = jnp.arange(slot_total) == 0

    def one_head(head_index):
        kv_head = head_index // group_width
        q_head = lax.dynamic_index_in_dim(q_tiles, head_index, axis=2, keepdims=False).astype(jnp.float32)
        k_head = lax.dynamic_index_in_dim(key_block_tiles, kv_head, axis=2, keepdims=False)
        v_head = lax.dynamic_index_in_dim(value_block_tiles, kv_head, axis=2, keepdims=False)
        offset_list = lax.dynamic_index_in_dim(slash_offsets, head_index, axis=0, keepdims=False)
        vert_list = lax.dynamic_index_in_dim(vert_blocks, head_index, axis=0, keepdims=False)
        targets = blocks[:, None] - offset_list[None, :]
        slash_ok = (offset_list[None, :] >= 1) & (targets >= 0)
        hits = slash_ok[:, :, None] & (targets[:, :, None] == vert_list[None, None, :])
        vert_ok = (vert_list[None, :] >= 0) & (vert_list[None, :] < blocks[:, None]) & jnp.logical_not(jnp.any(hits, axis=1))
        vert_full = jnp.broadcast_to(vert_list[None, :], (total_blocks, NV))
        chosen = jnp.concatenate([blocks[:, None], jnp.where(slash_ok, targets, 0), jnp.where(vert_ok, vert_full, 0)], axis=1).astype(jnp.int32)
        allowed = jnp.concatenate([jnp.ones((total_blocks, 1), dtype=bool), slash_ok, vert_ok], axis=1)
        k_sel = k_head[chosen].astype(jnp.float32)
        v_sel = v_head[chosen].astype(jnp.float32)
        scores = jnp.einsum("nqd,nskd->nqsk", q_head, k_sel) * score_scale
        keep_mask = allowed[:, None, :, None] & (causal[None, :, None, :] | jnp.logical_not(first_slot)[None, None, :, None])
        scores = jnp.where(keep_mask, scores, neg_large)
        row_best = jnp.max(scores, axis=(2, 3), keepdims=True)
        weights = jnp.where(keep_mask, jnp.exp(scores - row_best), 0.0)
        total = jnp.sum(weights, axis=(2, 3))
        probs_low = weights.astype(jnp.bfloat16).astype(jnp.float32)
        summed = jnp.einsum("nqsk,nskd->nqd", probs_low, v_sel)
        return (summed / total[:, :, None]).astype(jnp.bfloat16)

    heads_out = lax.map(one_head, jnp.arange(QUERY_HEADS, dtype=jnp.int32))
    return heads_out.transpose(1, 2, 0, 3).reshape(TOTAL_TOKENS, QUERY_HEADS * HEAD_SIZE)
```

```python
import functools

import jax
import jax.numpy as jnp
import numpy as np
from jax import lax
from jax.experimental import pallas as pl
from jax.experimental.pallas import tpu as pltpu
from jax.sharding import PartitionSpec as P

QUERY_HEADS = 64
KEY_VALUE_HEADS = 8
HEAD_SIZE = 128
BLOCK_TOKENS = 128


neg_large = -1e30


def passed_along(value, axis, steps):
    count = lax.axis_size(axis)
    initial, last = (max(0, -steps), min(count, count - steps))
    return lax.ppermute(value, axis, [(source, source + steps) for source in range(initial, last)])


def add_slot(running, slot_scores, allowed, weigh):
    best, total, accum = running
    slot_scores = jnp.where(allowed, slot_scores, neg_large)
    new_best = jnp.maximum(best, jnp.max(slot_scores, axis=-1))
    factor = jnp.exp(best - new_best)
    weights = jnp.where(allowed, jnp.exp(slot_scores - new_best[..., None]), 0.0)
    total = total * factor + jnp.sum(weights, axis=-1)
    accum = accum * factor[..., None] + weigh(weights.astype(jnp.bfloat16))
    return (new_best, total, accum)


def shards(queries, key_state_rows, value_state_rows, vert_blocks, slash_offsets):
    ulysses_count = lax.axis_size("uly")
    group_id = lax.axis_index("grp")
    uly_id = lax.axis_index("uly")
    per_device = QUERY_HEADS // ulysses_count
    group_width = QUERY_HEADS // KEY_VALUE_HEADS
    token_rows = queries.shape[0]
    ordering = jnp.arange(QUERY_HEADS, dtype=jnp.int32)
    heads_per_slot = np.arange(ulysses_count) * per_device // group_width
    key_outgoing = key_state_rows.reshape(token_rows, KEY_VALUE_HEADS, HEAD_SIZE)[
        :, heads_per_slot
    ].reshape(token_rows, ulysses_count * HEAD_SIZE)
    value_outgoing = value_state_rows.reshape(token_rows, KEY_VALUE_HEADS, HEAD_SIZE)[
        :, heads_per_slot
    ].reshape(token_rows, ulysses_count * HEAD_SIZE)
    q_group, k_group, v_group = (
        lax.all_to_all(queries, "uly", split_axis=1, concat_axis=0, tiled=True),
        lax.all_to_all(key_outgoing, "uly", split_axis=1, concat_axis=0, tiled=True),
        lax.all_to_all(value_outgoing, "uly", split_axis=1, concat_axis=0, tiled=True),
    )
    seg_rows = q_group.shape[0]
    block_count = seg_rows // BLOCK_TOKENS
    reach = block_count // 2
    q_tiles = q_group.reshape(block_count, BLOCK_TOKENS, per_device, HEAD_SIZE)
    key_block_tiles = k_group.reshape(block_count, BLOCK_TOKENS, HEAD_SIZE)
    value_block_tiles = v_group.reshape(block_count, BLOCK_TOKENS, HEAD_SIZE)
    prior_k, prior_v = passed_along(
        (key_block_tiles[block_count - reach :], value_block_tiles[block_count - reach :]), "grp", 1
    )
    k_wide = jnp.concatenate([prior_k, key_block_tiles], axis=0)
    v_wide = jnp.concatenate([prior_v, value_block_tiles], axis=0)
    heads_here = lax.dynamic_slice_in_dim(ordering, uly_id * per_device, per_device)
    vert_list = jnp.take(vert_blocks, heads_here, axis=0)
    offset_list = jnp.take(slash_offsets, heads_here, axis=0)
    local_block = jnp.where(vert_list >= 0, vert_list % block_count, 0)
    owned = (vert_list >= 0) & (vert_list // block_count == group_id)
    pick_k = jnp.where(
        owned[:, :, None, None], key_block_tiles[local_block], jnp.zeros((), jnp.bfloat16)
    )
    pick_v = jnp.where(
        owned[:, :, None, None], value_block_tiles[local_block], jnp.zeros((), jnp.bfloat16)
    )
    summed_k, summed_v = (
        lax.psum(pick_k.astype(jnp.float32).astype(jnp.bfloat16), "grp").astype(jnp.float32),
        lax.psum(pick_v.astype(jnp.float32).astype(jnp.bfloat16), "grp").astype(jnp.float32),
    )
    vert_k = summed_k.astype(jnp.bfloat16)
    vert_v = summed_v.astype(jnp.bfloat16)
    query_blocks = group_id * block_count + jnp.arange(block_count, dtype=jnp.int32)
    score_scale = HEAD_SIZE ** (-0.5)
    causal = (jnp.arange(BLOCK_TOKENS)[:, None] >= jnp.arange(BLOCK_TOKENS)[None, :])[
        None, :, None, :
    ]
    diag_scores = (
        jnp.einsum("nqhd,nkd->nqhk", q_tiles, key_block_tiles, preferred_element_type=jnp.float32)
        * score_scale
    )
    diag_scores = jnp.where(causal, diag_scores, neg_large)
    best = jnp.max(diag_scores, axis=-1)
    diag_weights = jnp.where(causal, jnp.exp(diag_scores - best[..., None]), 0.0)
    total = jnp.sum(diag_weights, axis=-1)
    accum = jnp.einsum(
        "nqhk,nkd->nqhd",
        diag_weights.astype(jnp.bfloat16),
        value_block_tiles,
        preferred_element_type=jnp.float32,
    )
    running = (best, total, accum)

    def slash_slot(slot_index, running):
        offset_now = lax.dynamic_index_in_dim(offset_list, slot_index, axis=1, keepdims=False)
        starts = jnp.where(offset_now >= 1, reach - offset_now, 0)

        def near_slice(begin_at):
            return (
                lax.dynamic_slice_in_dim(k_wide, begin_at, block_count, 0),
                lax.dynamic_slice_in_dim(v_wide, begin_at, block_count, 0),
            )

        k_near, v_near = jax.vmap(near_slice)(starts)
        allowed = (offset_now[None, :] >= 1) & (query_blocks[:, None] - offset_now[None, :] >= 0)
        slot_scores = (
            jnp.einsum("nqhd,hnkd->nqhk", q_tiles, k_near, preferred_element_type=jnp.float32)
            * score_scale
        )

        def weigh_near(prob_low):
            return jnp.einsum(
                "nqhk,hnkd->nqhd", prob_low, v_near, preferred_element_type=jnp.float32
            )

        return add_slot(running, slot_scores, allowed[:, None, :, None], weigh_near)

    slash_turns = jnp.max(jnp.sum((offset_list >= 1).astype(jnp.int32), axis=1))
    running = lax.fori_loop(0, slash_turns, slash_slot, running)

    def vert_slot(slot_index, running):
        block_now = lax.dynamic_index_in_dim(vert_list, slot_index, axis=1, keepdims=False)
        k_far = lax.dynamic_index_in_dim(vert_k, slot_index, axis=1, keepdims=False)
        v_far = lax.dynamic_index_in_dim(vert_v, slot_index, axis=1, keepdims=False)
        hits = (offset_list[None, :, :] >= 1) & (
            query_blocks[:, None, None] - offset_list[None, :, :] == block_now[None, :, None]
        )
        allowed = (
            (block_now[None, :] >= 0)
            & (block_now[None, :] < query_blocks[:, None])
            & jnp.logical_not(jnp.any(hits, axis=2))
        )
        slot_scores = (
            jnp.einsum("nqhd,hkd->nqhk", q_tiles, k_far, preferred_element_type=jnp.float32)
            * score_scale
        )

        def weigh_far(prob_low):
            return jnp.einsum("nqhk,hkd->nqhd", prob_low, v_far, preferred_element_type=jnp.float32)

        return add_slot(running, slot_scores, allowed[:, None, :, None], weigh_far)

    vert_turns = jnp.max(jnp.sum((vert_list >= 0).astype(jnp.int32), axis=1))
    best, total, accum = lax.fori_loop(0, vert_turns, vert_slot, running)
    mixed = (
        (accum / total[..., None]).astype(jnp.bfloat16).reshape(seg_rows, per_device * HEAD_SIZE)
    )
    returned = lax.all_to_all(mixed, "uly", split_axis=0, concat_axis=1, tiled=True)
    return returned


MESH = pl.DeviceIdType.MESH
LOG2_E = 1.4426950408889634
HALVES = 2
FOUR = 4
NEAR = ((0, 1), (1, 0), (1, 1))


def axis_pair(half):
    return ("y", "x") if half == 0 else ("x", "y")


def whereabouts(group, member):
    return {"x": group // 2, "core": group % 2, "y": member % 2, "z": member // 2}


def host_of(half, where):
    shared, _ = axis_pair(half)
    return where[shared] * 2 + where["core"]


def place_of(half, where, length):
    shared, other = axis_pair(half)
    major, minor = ("core", shared) if half == 0 else (shared, "core")
    return ((where[major] * length + where["z"]) * 2 + where[other]) * 2 + where[minor]


def place_table(group_count, uly_count):
    block = np.arange(group_count * uly_count)
    where = whereabouts(block // uly_count, block % uly_count)
    rows = [place_of(half, where, uly_count // 2) for half in range(HALVES)]
    return np.stack(rows).astype(np.int32)


def flipped(where, axis, by):
    return {**where, axis: 1 - where[axis]} if by else where


def attend(row, q_refs, k_buf, v_buf, place_ref, vert_ref, slash_ref, o_refs, q_head, turn, places):
    slash_slots, vert_slots = slash_ref.shape[0], vert_ref.shape[0]
    rate = HEAD_SIZE ** (-0.5) * LOG2_E
    causal = lax.broadcasted_iota(
        jnp.int32, (BLOCK_TOKENS, BLOCK_TOKENS), 0
    ) >= lax.broadcasted_iota(jnp.int32, (BLOCK_TOKENS, BLOCK_TOKENS), 1)
    columns = pl.ds(turn * HEAD_SIZE, HEAD_SIZE)
    offsets = [slash_ref[slot, q_head] for slot in range(slash_slots)]
    listed = [vert_ref[slot, q_head] for slot in range(vert_slots)]

    def slots_of(here):
        blocks, allowed = [here], [None]
        for offset in offsets:
            ok = (offset >= 1) & (here - offset >= 0)
            blocks.append(jnp.where(ok, here - offset, here))
            allowed.append(ok)
        for block in listed:
            ok = (block >= 0) & (block < here)
            for offset in offsets:
                ok = ok & jnp.logical_not((offset >= 1) & (here - offset == block))
            blocks.append(jnp.where(ok, block, here))
            allowed.append(ok)
        return blocks, allowed

    chosen_slots = [slots_of(here) for here in places]
    scores, probs, totals = [], [], []
    for q_ref, (blocks, _) in zip(q_refs, chosen_slots):
        keys = jnp.concatenate([k_buf[place_ref[row, block]] for block in blocks], axis=0)
        scores.append(
            lax.dot_general(
                q_ref[:, columns],
                keys,
                (((1,), (1,)), ((), ())),
                preferred_element_type=jnp.float32,
            )
        )
    for score, (_, allowed) in zip(scores, chosen_slots):
        pieces = []
        for slot, ok in enumerate(allowed):
            piece = score[:, slot * BLOCK_TOKENS : (slot + 1) * BLOCK_TOKENS]
            if ok is None:
                pieces.append(jnp.where(causal, piece, neg_large))
            else:
                pieces.append(piece + jnp.where(ok, 0.0, neg_large).astype(jnp.float32))
        best = functools.reduce(jnp.maximum, pieces)
        best = jnp.max(best, axis=1, keepdims=True)
        weights = [jnp.exp2((piece - best) * rate) for piece in pieces]
        total = functools.reduce(jnp.add, weights)
        totals.append(jnp.sum(total, axis=1, keepdims=True))
        probs.append(jnp.concatenate([weight.astype(jnp.bfloat16) for weight in weights], axis=1))
    for o_ref, prob, total, (blocks, _) in zip(o_refs, probs, totals, chosen_slots):
        values = jnp.concatenate([v_buf[place_ref[row, block]] for block in blocks], axis=0)
        mixed = jnp.dot(prob, values, preferred_element_type=jnp.float32)
        o_ref[:, columns] = (mixed / total).astype(o_ref.dtype)


def split_kernel(
    uly_count,
    place_ref,
    vert_ref,
    slash_ref,
    q_hbm,
    k_hbm,
    v_hbm,
    out_hbm,
    k_own,
    v_own,
    load_sem,
    own_sem,
    ex_send,
    ex_recv,
    q_sem,
    q_send,
    q_recv,
    g_send,
    g_recv,
    o_sem,
    o_send,
    o_recv,
    *buffers,
):
    length = uly_count // 2
    group, member = lax.axis_index("grp"), lax.axis_index("uly")
    me = whereabouts(group, member)
    z = me["z"]
    per_kv = q_hbm.shape[1] // KEY_VALUE_HEADS
    turns = per_kv // HEAD_SIZE
    held = buffers[:4]
    q_bufs = (buffers[4:8], buffers[8:12])
    o_bufs = (buffers[12:16], buffers[16:20])
    sources = (k_own, v_own)

    def block_at(where):
        return (where["x"] * 2 + where["core"]) * uly_count + where["z"] * 2 + where["y"]

    def device_at(where):
        return (where["x"] * 2 + where["core"], where["z"] * 2 + where["y"])

    def relative(half, steps):
        shared, _ = axis_pair(half)
        return flipped(flipped(me, shared, steps[0]), "core", steps[1])

    def kv_head(half, where):
        return half * FOUR + host_of(half, where)

    def lanes(start, width):
        return pl.ds(pl.multiple_of(start, HEAD_SIZE), width)

    loads = []
    for n, (source, target) in enumerate(((k_hbm, k_own), (v_hbm, v_own))):
        loads.append(pltpu.make_async_copy(source, target, load_sem.at[n]))
        loads[-1].start()
    own = []
    for half in range(HALVES):
        for kind, source in enumerate((k_hbm, v_hbm)):
            item = 2 * half + kind
            columns = lanes(kv_head(half, me) * HEAD_SIZE, HEAD_SIZE)
            own.append(
                pltpu.make_async_copy(
                    source.at[:, columns],
                    held[item].at[place_of(half, me, length)],
                    own_sem.at[item],
                )
            )
            own[-1].start()
    q_own = []
    for half in range(HALVES):
        columns = lanes(kv_head(half, me) * per_kv, per_kv)
        q_own.append(
            pltpu.make_async_copy(q_hbm.at[:, columns], q_bufs[half][0], q_sem.at[half])
        )
        q_own[-1].start()

    barrier = pltpu.get_barrier_semaphore()
    around = [relative(half, steps) for half in range(HALVES) for steps in NEAR]
    around = around[:3] + around[4:]
    for where in around:
        pl.semaphore_signal(barrier, inc=1, device_id=device_at(where), device_id_type=MESH)

    def greet(step):
        pl.semaphore_signal(
            barrier, inc=1, device_id=device_at({**me, "z": z + step}), device_id_type=MESH
        )

    pl.when(z > 0)(lambda: greet(-1))
    pl.when(z < length - 1)(lambda: greet(1))
    count = len(around) + jnp.where(z > 0, 1, 0) + jnp.where(z < length - 1, 1, 0)
    pl.semaphore_wait(barrier, count)
    for load in loads:
        load.wait()

    def remote(source, target, send, recv, where):
        return pltpu.make_async_remote_copy(
            src_ref=source,
            dst_ref=target,
            send_sem=send,
            recv_sem=recv,
            device_id=device_at(where),
            device_id_type=MESH,
        )

    sent = []

    def begin(copy):
        copy.start()
        sent.append(copy)
        return copy

    exchanged = {}

    def exchange(half):
        for kind in range(2):
            item = 2 * half + kind
            for n, steps in enumerate(NEAR):
                peer = relative(half, steps)
                columns = lanes(kv_head(half, peer) * HEAD_SIZE, HEAD_SIZE)
                exchanged[item, n] = begin(
                    remote(
                        sources[kind].at[:, columns],
                        held[item].at[place_of(half, me, length)],
                        ex_send.at[item, n],
                        ex_recv.at[item, n],
                        peer,
                    )
                )

    asked = {}

    def ask(half):
        for n, steps in enumerate(NEAR):
            peer = relative(half, steps)
            columns = lanes(kv_head(half, peer) * per_kv, per_kv)
            asked[half, n] = begin(
                remote(
                    q_hbm.at[:, columns],
                    q_bufs[half][n + 1],
                    q_send.at[half, n],
                    q_recv.at[half, n],
                    peer,
                )
            )

    def hop(item, major, slab, way):
        half = item // 2
        _, other = axis_pair(half)
        first = ((major * length + slab) * 2 + me[other]) * 2
        part = held[item].at[pl.ds(first, 2)]
        if way == 2:
            where, lane = {**me, other: 1 - me[other]}, 1
        else:
            where, lane = {**me, "z": z + (1 if way == 0 else -1)}, 0
        return remote(
            part, part, g_send.at[item, major, slab, way], g_recv.at[item, major, slab, lane], where
        )

    def arrived(item, major, slab, lane):
        half = item // 2
        _, other = axis_pair(half)
        side = me[other] if lane == 0 else 1 - me[other]
        first = ((major * length + slab) * 2 + side) * 2
        part = held[item].at[pl.ds(first, 2)]
        remote(
            part, part, g_send.at[item, major, slab, 0], g_recv.at[item, major, slab, lane], me
        ).wait_recv()

    def ways(item, kind):
        up = (0, z < length - 1)
        down = (1, z > 0)
        across = (2, None if item >= 2 else me["x"] == 0)
        return {"own": (up, down, across), "below": (up, across), "above": (down, across)}[kind]

    def each_way(item, major, slab, kind, act):
        for way, ok in ways(item, kind):
            if ok is None:
                act(hop(item, major, slab, way))
            else:
                pl.when(ok)(lambda way=way: act(hop(item, major, slab, way)))

    def start(item, major, slab, kind):
        each_way(item, major, slab, kind, lambda copy: copy.start())

    def launch(item):
        own[item].wait()
        for n in range(len(NEAR)):
            exchanged[item, n].wait_recv()
        for major in range(2):
            start(item, major, z, "own")

    def step(item, major, distance):
        @pl.when(z >= distance)
        def _():
            arrived(item, major, z - distance, 0)
            start(item, major, z - distance, "below")

        @pl.when(z + distance < length)
        def _():
            arrived(item, major, z + distance, 0)
            start(item, major, z + distance, "above")

    def settle(item):
        def crossing():
            for major in range(2):
                for slab in range(length):
                    arrived(item, major, slab, 1)

        if item >= 2:
            crossing()
        else:
            pl.when(me["x"] == 1)(crossing)

    def drain(item):
        for major in range(2):
            each_way(item, major, z, "own", lambda copy: copy.wait_send())
            for distance in range(1, length):
                @pl.when(z >= distance)
                def _():
                    each_way(
                        item, major, z - distance, "below", lambda copy: copy.wait_send()
                    )

                @pl.when(z + distance < length)
                def _():
                    each_way(
                        item, major, z + distance, "above", lambda copy: copy.wait_send()
                    )

    answered = []

    def answer(half, turn):
        columns = lanes(kv_head(half, me) * per_kv + turn * HEAD_SIZE, HEAD_SIZE)
        local = pl.ds(turn * HEAD_SIZE, HEAD_SIZE)
        for n, steps in enumerate(NEAR):
            copy = begin(
                remote(
                    o_bufs[half][n + 1].at[:, local],
                    out_hbm.at[:, columns],
                    o_send.at[half, turn, n],
                    o_recv.at[half, turn, n],
                    relative(half, steps),
                )
            )
            answered.append(copy)
        copy = pltpu.make_async_copy(
            o_bufs[half][0].at[:, local], out_hbm.at[:, columns], o_sem.at[half, turn]
        )
        copy.start()
        own_out.append(copy)

    own_out = []
    where_from = ((0, 0),) + NEAR

    def compute(half, turn):
        places = [block_at(relative(half, steps)) for steps in where_from]
        attend(
            half,
            q_bufs[half],
            held[2 * half],
            held[2 * half + 1],
            place_ref,
            vert_ref,
            slash_ref,
            o_bufs[half],
            kv_head(half, me) * turns + turn,
            turn,
            places,
        )
        answer(half, turn)

    def steps_of(half, distance):
        return [(2 * half + kind, major, distance) for kind in range(2) for major in range(2)]

    exchange(0)
    exchange(1)
    ask(0)
    launch(0)
    launch(1)
    for distance in range(1, length - 1):
        for args in steps_of(0, distance):
            step(*args)
    launch(2)
    launch(3)
    for args in steps_of(0, length - 1):
        step(*args)
    ask(1)
    pending = [args for distance in range(1, length) for args in steps_of(1, distance)]
    for args in pending[:2]:
        step(*args)
    pending = pending[2:]
    settle(0)
    settle(1)
    q_own[0].wait()
    for n in range(len(NEAR)):
        asked[0, n].wait_recv()
    for turn in range(turns):
        compute(0, turn)
        for args in pending[:1]:
            step(*args)
        pending = pending[1:]
    for args in pending:
        step(*args)
    settle(2)
    settle(3)
    q_own[1].wait()
    for n in range(len(NEAR)):
        asked[1, n].wait_recv()
    for turn in range(turns):
        compute(1, turn)
    for copy in sent:
        copy.wait_send()
    for item in range(4):
        drain(item)
    for copy in answered:
        copy.wait_recv()
    for copy in own_out:
        copy.wait()


def split_shards(queries, key_state_rows, value_state_rows, vert_blocks, slash_offsets):
    group_count, uly_count = lax.axis_size("grp"), lax.axis_size("uly")
    blocks = group_count * uly_count
    length = uly_count // 2
    turns = QUERY_HEADS // KEY_VALUE_HEADS
    near = len(NEAR)
    dtype = queries.dtype
    smem = pl.BlockSpec(memory_space=pltpu.SMEM)
    hbm = pl.BlockSpec(memory_space=pl.ANY)
    dma = pltpu.SemaphoreType.DMA
    share = (BLOCK_TOKENS, turns * HEAD_SIZE)
    return pl.pallas_call(
        functools.partial(split_kernel, uly_count),
        out_shape=jax.ShapeDtypeStruct(queries.shape, dtype),
        in_specs=[smem, smem, smem, hbm, hbm, hbm],
        out_specs=hbm,
        scratch_shapes=[
            pltpu.VMEM(key_state_rows.shape, dtype),
            pltpu.VMEM(value_state_rows.shape, dtype),
            dma((2,)),
            dma((4,)),
            dma((4, near)),
            dma((4, near)),
            dma((HALVES,)),
            dma((HALVES, near)),
            dma((HALVES, near)),
            dma((4, 2, length, 3)),
            dma((4, 2, length, 2)),
            dma((HALVES, turns)),
            dma((HALVES, turns, near)),
            dma((HALVES, turns, near)),
        ]
        + [pltpu.VMEM((blocks, BLOCK_TOKENS, HEAD_SIZE), dtype)] * 4
        + [pltpu.VMEM(share, dtype)] * (4 * HALVES * 2),
        compiler_params=pltpu.CompilerParams(collective_id=0, has_side_effects=True),
        name="split_and_attend",
    )(
        jnp.asarray(place_table(group_count, uly_count)),
        vert_blocks.T,
        slash_offsets.T,
        queries,
        key_state_rows,
        value_state_rows,
    )


def chosen(queries, key_state_rows, *rest):
    group_count, uly_count = lax.axis_size("grp"), lax.axis_size("uly")
    fits = (
        group_count == FOUR
        and uly_count == 2 * FOUR
        and KEY_VALUE_HEADS == HALVES * FOUR
        and queries.shape[0] == BLOCK_TOKENS
    )
    plan = split_shards if fits else shards
    return plan(queries, key_state_rows, *rest)


def solution(mesh):
    return jax.shard_map(
        chosen,
        mesh=mesh,
        in_specs=(
            P(("grp", "uly"), None),
            P(("grp", "uly"), None),
            P(("grp", "uly"), None),
            P(),
            P(),
        ),
        out_specs=P(("grp", "uly"), None),
        check_vma=False,
    )
```

```python
import functools

import jax
import jax.numpy as jnp
import numpy as np
from jax import lax
from jax.experimental import pallas as pl
from jax.experimental.pallas import tpu as pltpu
from jax.sharding import PartitionSpec as P

QUERY_HEADS = 64
KEY_VALUE_HEADS = 8
HEAD_SIZE = 128
BLOCK_TOKENS = 128


neg_large = -1e30


def passed_along(value, axis, steps):
    count = lax.axis_size(axis)
    initial, last = (max(0, -steps), min(count, count - steps))
    return lax.ppermute(value, axis, [(source, source + steps) for source in range(initial, last)])


def add_slot(running, slot_scores, allowed, weigh):
    best, total, accum = running
    slot_scores = jnp.where(allowed, slot_scores, neg_large)
    new_best = jnp.maximum(best, jnp.max(slot_scores, axis=-1))
    factor = jnp.exp(best - new_best)
    weights = jnp.where(allowed, jnp.exp(slot_scores - new_best[..., None]), 0.0)
    total = total * factor + jnp.sum(weights, axis=-1)
    accum = accum * factor[..., None] + weigh(weights.astype(jnp.bfloat16))
    return (new_best, total, accum)


def shards(queries, key_state_rows, value_state_rows, vert_blocks, slash_offsets):
    ulysses_count = lax.axis_size("uly")
    group_id = lax.axis_index("grp")
    uly_id = lax.axis_index("uly")
    per_device = QUERY_HEADS // ulysses_count
    group_width = QUERY_HEADS // KEY_VALUE_HEADS
    token_rows = queries.shape[0]
    ordering = jnp.arange(QUERY_HEADS, dtype=jnp.int32)
    heads_per_slot = np.arange(ulysses_count) * per_device // group_width
    key_outgoing = key_state_rows.reshape(token_rows, KEY_VALUE_HEADS, HEAD_SIZE)[
        :, heads_per_slot
    ].reshape(token_rows, ulysses_count * HEAD_SIZE)
    value_outgoing = value_state_rows.reshape(token_rows, KEY_VALUE_HEADS, HEAD_SIZE)[
        :, heads_per_slot
    ].reshape(token_rows, ulysses_count * HEAD_SIZE)
    q_group, k_group, v_group = (
        lax.all_to_all(queries, "uly", split_axis=1, concat_axis=0, tiled=True),
        lax.all_to_all(key_outgoing, "uly", split_axis=1, concat_axis=0, tiled=True),
        lax.all_to_all(value_outgoing, "uly", split_axis=1, concat_axis=0, tiled=True),
    )
    seg_rows = q_group.shape[0]
    block_count = seg_rows // BLOCK_TOKENS
    reach = block_count // 2
    q_tiles = q_group.reshape(block_count, BLOCK_TOKENS, per_device, HEAD_SIZE)
    key_block_tiles = k_group.reshape(block_count, BLOCK_TOKENS, HEAD_SIZE)
    value_block_tiles = v_group.reshape(block_count, BLOCK_TOKENS, HEAD_SIZE)
    prior_k, prior_v = passed_along(
        (key_block_tiles[block_count - reach :], value_block_tiles[block_count - reach :]), "grp", 1
    )
    k_wide = jnp.concatenate([prior_k, key_block_tiles], axis=0)
    v_wide = jnp.concatenate([prior_v, value_block_tiles], axis=0)
    heads_here = lax.dynamic_slice_in_dim(ordering, uly_id * per_device, per_device)
    vert_list = jnp.take(vert_blocks, heads_here, axis=0)
    offset_list = jnp.take(slash_offsets, heads_here, axis=0)
    local_block = jnp.where(vert_list >= 0, vert_list % block_count, 0)
    owned = (vert_list >= 0) & (vert_list // block_count == group_id)
    pick_k = jnp.where(
        owned[:, :, None, None], key_block_tiles[local_block], jnp.zeros((), jnp.bfloat16)
    )
    pick_v = jnp.where(
        owned[:, :, None, None], value_block_tiles[local_block], jnp.zeros((), jnp.bfloat16)
    )
    summed_k, summed_v = (
        lax.psum(pick_k.astype(jnp.float32).astype(jnp.bfloat16), "grp").astype(jnp.float32),
        lax.psum(pick_v.astype(jnp.float32).astype(jnp.bfloat16), "grp").astype(jnp.float32),
    )
    vert_k = summed_k.astype(jnp.bfloat16)
    vert_v = summed_v.astype(jnp.bfloat16)
    query_blocks = group_id * block_count + jnp.arange(block_count, dtype=jnp.int32)
    score_scale = HEAD_SIZE ** (-0.5)
    causal = (jnp.arange(BLOCK_TOKENS)[:, None] >= jnp.arange(BLOCK_TOKENS)[None, :])[
        None, :, None, :
    ]
    diag_scores = (
        jnp.einsum("nqhd,nkd->nqhk", q_tiles, key_block_tiles, preferred_element_type=jnp.float32)
        * score_scale
    )
    diag_scores = jnp.where(causal, diag_scores, neg_large)
    best = jnp.max(diag_scores, axis=-1)
    diag_weights = jnp.where(causal, jnp.exp(diag_scores - best[..., None]), 0.0)
    total = jnp.sum(diag_weights, axis=-1)
    accum = jnp.einsum(
        "nqhk,nkd->nqhd",
        diag_weights.astype(jnp.bfloat16),
        value_block_tiles,
        preferred_element_type=jnp.float32,
    )
    running = (best, total, accum)

    def slash_slot(slot_index, running):
        offset_now = lax.dynamic_index_in_dim(offset_list, slot_index, axis=1, keepdims=False)
        starts = jnp.where(offset_now >= 1, reach - offset_now, 0)

        def near_slice(begin_at):
            return (
                lax.dynamic_slice_in_dim(k_wide, begin_at, block_count, 0),
                lax.dynamic_slice_in_dim(v_wide, begin_at, block_count, 0),
            )

        k_near, v_near = jax.vmap(near_slice)(starts)
        allowed = (offset_now[None, :] >= 1) & (query_blocks[:, None] - offset_now[None, :] >= 0)
        slot_scores = (
            jnp.einsum("nqhd,hnkd->nqhk", q_tiles, k_near, preferred_element_type=jnp.float32)
            * score_scale
        )

        def weigh_near(prob_low):
            return jnp.einsum(
                "nqhk,hnkd->nqhd", prob_low, v_near, preferred_element_type=jnp.float32
            )

        return add_slot(running, slot_scores, allowed[:, None, :, None], weigh_near)

    slash_turns = jnp.max(jnp.sum((offset_list >= 1).astype(jnp.int32), axis=1))
    running = lax.fori_loop(0, slash_turns, slash_slot, running)

    def vert_slot(slot_index, running):
        block_now = lax.dynamic_index_in_dim(vert_list, slot_index, axis=1, keepdims=False)
        k_far = lax.dynamic_index_in_dim(vert_k, slot_index, axis=1, keepdims=False)
        v_far = lax.dynamic_index_in_dim(vert_v, slot_index, axis=1, keepdims=False)
        hits = (offset_list[None, :, :] >= 1) & (
            query_blocks[:, None, None] - offset_list[None, :, :] == block_now[None, :, None]
        )
        allowed = (
            (block_now[None, :] >= 0)
            & (block_now[None, :] < query_blocks[:, None])
            & jnp.logical_not(jnp.any(hits, axis=2))
        )
        slot_scores = (
            jnp.einsum("nqhd,hkd->nqhk", q_tiles, k_far, preferred_element_type=jnp.float32)
            * score_scale
        )

        def weigh_far(prob_low):
            return jnp.einsum("nqhk,hkd->nqhd", prob_low, v_far, preferred_element_type=jnp.float32)

        return add_slot(running, slot_scores, allowed[:, None, :, None], weigh_far)

    vert_turns = jnp.max(jnp.sum((vert_list >= 0).astype(jnp.int32), axis=1))
    best, total, accum = lax.fori_loop(0, vert_turns, vert_slot, running)
    mixed = (
        (accum / total[..., None]).astype(jnp.bfloat16).reshape(seg_rows, per_device * HEAD_SIZE)
    )
    returned = lax.all_to_all(mixed, "uly", split_axis=0, concat_axis=1, tiled=True)
    return returned


MESH = pl.DeviceIdType.MESH
LOG2_E = 1.4426950408889634
HALVES = 2
PHASES = ((0, 0), (1, 0), (0, 1), (1, 1))
UP, DOWN, ACROSS, BESIDE, BESIDE_TOO = range(5)
GANG = 2


def axis_pair(half):
    return ("y", "x") if half == 0 else ("x", "y")


def whereabouts(group, member):
    return {"x": group // 2, "core": group % 2, "y": member % 2, "z": member // 2}


def flipped(where, axis):
    return {**where, axis: 1 - where[axis]}


def place_of(half, where, length):
    shared, other = axis_pair(half)
    return ((where["core"] * length + where["z"]) * 2 + where[other]) * 2 + where[shared]


def place_table(group_count, uly_count):
    block = np.arange(group_count * uly_count)
    where = whereabouts(block // uly_count, block % uly_count)
    rows = [place_of(half, where, uly_count // 2) for half in range(HALVES)]
    return np.stack(rows).astype(np.int32)


def attend(row, units, k_buf, v_buf, place_ref, vert_ref, slash_ref):
    slash_slots, vert_slots = slash_ref.shape[0], vert_ref.shape[0]
    rate = HEAD_SIZE ** (-0.5) * LOG2_E
    causal = lax.broadcasted_iota(
        jnp.int32, (BLOCK_TOKENS, BLOCK_TOKENS), 0
    ) >= lax.broadcasted_iota(jnp.int32, (BLOCK_TOKENS, BLOCK_TOKENS), 1)

    def slots_of(q_head, here):
        blocks, allowed = [here], [None]
        offsets = [slash_ref[slot, q_head] for slot in range(slash_slots)]
        for offset in offsets:
            ok = (offset >= 1) & (here - offset >= 0)
            blocks.append(jnp.where(ok, here - offset, here))
            allowed.append(ok)
        for slot in range(vert_slots):
            block = vert_ref[slot, q_head]
            ok = (block >= 0) & (block < here)
            for offset in offsets:
                ok = ok & jnp.logical_not((offset >= 1) & (here - offset == block))
            blocks.append(jnp.where(ok, block, here))
            allowed.append(ok)
        return blocks, allowed

    chosen_slots = [slots_of(q_head, here) for _, _, _, q_head, here in units]
    scores, probs, totals = [], [], []
    for (q_ref, _, columns, _, _), (blocks, _) in zip(units, chosen_slots):
        keys = jnp.concatenate([k_buf[place_ref[row, block]] for block in blocks], axis=0)
        scores.append(
            lax.dot_general(
                q_ref[:, columns],
                keys,
                (((1,), (1,)), ((), ())),
                preferred_element_type=jnp.float32,
            )
        )
    for score, (_, allowed) in zip(scores, chosen_slots):
        pieces = []
        for slot, ok in enumerate(allowed):
            piece = score[:, slot * BLOCK_TOKENS : (slot + 1) * BLOCK_TOKENS]
            if ok is None:
                pieces.append(jnp.where(causal, piece, neg_large))
            else:
                pieces.append(piece + jnp.where(ok, 0.0, neg_large).astype(jnp.float32))
        best = functools.reduce(jnp.maximum, pieces)
        best = jnp.max(best, axis=1, keepdims=True)
        weights = [jnp.exp2((piece - best) * rate) for piece in pieces]
        total = functools.reduce(jnp.add, weights)
        totals.append(jnp.sum(total, axis=1, keepdims=True))
        probs.append(jnp.concatenate([weight.astype(jnp.bfloat16) for weight in weights], axis=1))
    for (_, o_ref, columns, _, _), prob, total, (blocks, _) in zip(
        units, probs, totals, chosen_slots
    ):
        values = jnp.concatenate([v_buf[place_ref[row, block]] for block in blocks], axis=0)
        mixed = jnp.dot(prob, values, preferred_element_type=jnp.float32)
        o_ref[:, columns] = (mixed / total).astype(o_ref.dtype)


def split_kernel(
    uly_count,
    place_ref,
    vert_ref,
    slash_ref,
    q_hbm,
    k_hbm,
    v_hbm,
    out_hbm,
    k_own,
    v_own,
    load_sem,
    own_sem,
    ex_send,
    ex_recv,
    q_sem,
    q_send,
    q_recv,
    g_send,
    g_recv,
    b_recv,
    o_sem,
    o_send,
    o_recv,
    *buffers,
):
    length = uly_count // 2
    group, member = lax.axis_index("grp"), lax.axis_index("uly")
    me = whereabouts(group, member)
    z = me["z"]
    per_kv = q_hbm.shape[1] // KEY_VALUE_HEADS
    turns = per_kv // HEAD_SIZE
    gangs = turns // GANG
    held = buffers[:8]
    q_bufs = [buffers[8 + 2 * n : 10 + 2 * n] for n in range(4)]
    o_bufs = [buffers[16 + 2 * n : 18 + 2 * n] for n in range(4)]
    sources = (k_own, v_own)

    def block_at(where):
        return (where["x"] * 2 + where["core"]) * uly_count + where["z"] * 2 + where["y"]

    def device_at(where):
        return (where["x"] * 2 + where["core"], where["z"] * 2 + where["y"])

    def partner(half):
        return flipped(me, axis_pair(half)[0])

    def kv_head(half, n, where):
        return (half * 2 + where[axis_pair(half)[0]]) * 2 + n

    def lanes(start, width):
        return pl.ds(pl.multiple_of(start, HEAD_SIZE), width)

    loads = []
    for n, (source, target) in enumerate(((k_hbm, k_own), (v_hbm, v_own))):
        loads.append(pltpu.make_async_copy(source, target, load_sem.at[n]))
        loads[-1].start()
    own, q_own = {}, {}
    for half, n in PHASES:
        for kind, source in enumerate((k_hbm, v_hbm)):
            item = (half * 2 + n) * 2 + kind
            columns = lanes(kv_head(half, n, me) * HEAD_SIZE, HEAD_SIZE)
            own[item] = pltpu.make_async_copy(
                source.at[:, columns], held[item].at[place_of(half, me, length)], own_sem.at[item]
            )
            own[item].start()
    for half, n in PHASES:
        columns = lanes(kv_head(half, n, me) * per_kv, per_kv)
        q_own[half, n] = pltpu.make_async_copy(
            q_hbm.at[:, columns], q_bufs[half * 2 + n][0], q_sem.at[half * 2 + n]
        )
        q_own[half, n].start()

    barrier = pltpu.get_barrier_semaphore()
    around = [flipped(me, axis) for axis in ("x", "y", "core")]
    for where in around:
        pl.semaphore_signal(barrier, inc=1, device_id=device_at(where), device_id_type=MESH)

    def greet(step):
        pl.semaphore_signal(
            barrier, inc=1, device_id=device_at({**me, "z": z + step}), device_id_type=MESH
        )

    pl.when(z > 0)(lambda: greet(-1))
    pl.when(z < length - 1)(lambda: greet(1))
    count = len(around) + jnp.where(z > 0, 1, 0) + jnp.where(z < length - 1, 1, 0)
    pl.semaphore_wait(barrier, count)
    for load in loads:
        load.wait()

    def remote(source, target, send, recv, where):
        return pltpu.make_async_remote_copy(
            src_ref=source,
            dst_ref=target,
            send_sem=send,
            recv_sem=recv,
            device_id=device_at(where),
            device_id_type=MESH,
        )

    sent = []

    def begin(copy):
        copy.start()
        sent.append(copy)
        return copy

    exchanged, asked, answered, own_out = {}, {}, [], []

    def exchange(half, n):
        peer = partner(half)
        columns = lanes(kv_head(half, n, peer) * HEAD_SIZE, HEAD_SIZE)
        for kind in range(2):
            item = (half * 2 + n) * 2 + kind
            exchanged[item] = begin(
                remote(
                    sources[kind].at[:, columns],
                    held[item].at[place_of(half, me, length)],
                    ex_send.at[item],
                    ex_recv.at[item],
                    peer,
                )
            )

    def ask(half, n):
        peer = partner(half)
        columns = lanes(kv_head(half, n, peer) * per_kv, per_kv)
        asked[half, n] = begin(
            remote(
                q_hbm.at[:, columns],
                q_bufs[half * 2 + n][1],
                q_send.at[half * 2 + n],
                q_recv.at[half * 2 + n],
                peer,
            )
        )

    def part_of(item, core, slab, lane):
        other = axis_pair(item // 4)[1]
        side = me[other] if lane == 0 else 1 - me[other]
        return held[item].at[pl.ds(((core * length + slab) * 2 + side) * 2, 2)]

    def hop(item, slab, way):
        other = axis_pair(item // 4)[1]
        lane = 1 if way == BESIDE_TOO else 0
        part = part_of(item, me["core"], slab, lane)
        if way in (BESIDE, BESIDE_TOO):
            where, recv = flipped(me, "core"), b_recv.at[item, slab, lane]
        elif way == ACROSS:
            where, recv = flipped(me, other), g_recv.at[item, slab, 1]
        else:
            where, recv = {**me, "z": z + (1 if way == UP else -1)}, g_recv.at[item, slab, 0]
        return remote(part, part, g_send.at[item, slab, way], recv, where)

    def wait_for(item, slab, lane):
        part = part_of(item, me["core"], slab, lane)
        recv = g_recv.at[item, slab, lane]
        remote(part, part, g_send.at[item, slab, 0], recv, me).wait_recv()

    def wait_beside(item, slab, lane):
        part = part_of(item, 1 - me["core"], slab, lane)
        recv = b_recv.at[item, slab, lane]
        remote(part, part, g_send.at[item, slab, 0], recv, me).wait_recv()

    def each_way(item, slab, ways, act):
        for way in ways:
            ok = {
                UP: z < length - 1,
                DOWN: z > 0,
                ACROSS: None if item >= 4 else me["x"] == 0,
                BESIDE: None,
                BESIDE_TOO: None,
            }[way]
            if ok is None:
                act(hop(item, slab, way))
            else:
                pl.when(ok)(lambda way=way: act(hop(item, slab, way)))

    def started(copy):
        copy.start()

    def finished(copy):
        copy.wait_send()

    def visit(item, distance, act, wait=False):
        if distance == 0:
            each_way(item, z, (UP, DOWN, ACROSS, BESIDE), act)
            return

        @pl.when(z >= distance)
        def _():
            if wait:
                wait_for(item, z - distance, 0)
            each_way(item, z - distance, (UP, ACROSS, BESIDE), act)

        @pl.when(z + distance < length)
        def _():
            if wait:
                wait_for(item, z + distance, 0)
            each_way(item, z + distance, (DOWN, ACROSS, BESIDE), act)

    def crossed(item):
        return lambda body: body() if item >= 4 else pl.when(me["x"] == 1)(body)

    def items_of(phase):
        half, n = PHASES[phase]
        return [(half * 2 + n) * 2 + kind for kind in range(2)]

    def launch(item):
        own[item].wait()
        exchanged[item].wait_recv()
        visit(item, 0, started)

    def step(item, distance):
        if distance == 0:
            launch(item)
        else:
            visit(item, distance, started, wait=True)

    def steps(phase, distance):
        return [(item, distance) for item in items_of(phase)]

    def settle(phase):
        for item in items_of(phase):
            @crossed(item)
            def _():
                for slab in range(length):
                    wait_for(item, slab, 1)
                    each_way(item, slab, (BESIDE_TOO,), started)

        for item in items_of(phase):
            for slab in range(length):
                wait_beside(item, slab, 0)

            @crossed(item)
            def _():
                for slab in range(length):
                    wait_beside(item, slab, 1)

        q_own[PHASES[phase]].wait()
        asked[PHASES[phase]].wait_recv()

    def drain(item):
        for distance in range(length):
            visit(item, distance, finished)

        @crossed(item)
        def _():
            for slab in range(length):
                each_way(item, slab, (BESIDE_TOO,), finished)

    def answer(phase, gang):
        half, n = PHASES[phase]
        index = half * 2 + n
        width = GANG * HEAD_SIZE
        columns = lanes(kv_head(half, n, me) * per_kv + gang * width, width)
        local = pl.ds(gang * width, width)
        copy = begin(
            remote(
                o_bufs[index][1].at[:, local],
                out_hbm.at[:, columns],
                o_send.at[index, gang],
                o_recv.at[index, gang],
                partner(half),
            )
        )
        answered.append(copy)
        copy = pltpu.make_async_copy(
            o_bufs[index][0].at[:, local], out_hbm.at[:, columns], o_sem.at[index, gang]
        )
        copy.start()
        own_out.append(copy)

    def compute(phase, gang):
        half, n = PHASES[phase]
        index = half * 2 + n
        units = []
        for turn in range(gang * GANG, (gang + 1) * GANG):
            for side, where in enumerate((me, partner(half))):
                units.append(
                    (
                        q_bufs[index][side],
                        o_bufs[index][side],
                        pl.ds(turn * HEAD_SIZE, HEAD_SIZE),
                        kv_head(half, n, me) * turns + turn,
                        block_at(where),
                    )
                )
        k_item, v_item = items_of(phase)
        attend(half, units, held[k_item], held[v_item], place_ref, vert_ref, slash_ref)

    def run(todo):
        for item, distance in todo:
            step(item, distance)

    for phase in range(4):
        exchange(*PHASES[phase])
    ask(0, 0)
    ask(0, 1)
    run(steps(0, 0) + steps(0, 1))
    run(steps(1, 0) + steps(0, 2) + steps(1, 1) + steps(0, 3))
    ask(1, 0)
    run(steps(2, 0) + steps(1, 2) + steps(2, 1) + steps(1, 3))
    later = [
        steps(3, 0) + steps(2, 2) + steps(3, 1)[:1],
        steps(3, 1)[1:] + steps(2, 3) + steps(3, 2)[:1],
        steps(3, 2)[1:] + steps(3, 3),
    ]
    for phase in range(4):
        settle(phase)
        todo = later[phase] if phase < 3 else []
        if phase == 2:
            ask(1, 1)
        for gang in range(gangs):
            compute(phase, gang)
            share = -(-len(todo) // (gangs - gang))
            run(todo[:share])
            todo = todo[share:]
            if phase != 2:
                answer(phase, gang)
        if phase == 2:
            for gang in range(gangs):
                answer(phase, gang)
    for copy in sent:
        copy.wait_send()
    for item in range(8):
        drain(item)
    for copy in answered:
        copy.wait_recv()
    for copy in own_out:
        copy.wait()


def split_shards(queries, key_state_rows, value_state_rows, vert_blocks, slash_offsets):
    group_count, uly_count = lax.axis_size("grp"), lax.axis_size("uly")
    blocks = group_count * uly_count
    length = uly_count // 2
    turns = QUERY_HEADS // KEY_VALUE_HEADS
    dtype = queries.dtype
    smem = pl.BlockSpec(memory_space=pltpu.SMEM)
    hbm = pl.BlockSpec(memory_space=pl.ANY)
    dma = pltpu.SemaphoreType.DMA
    share = (BLOCK_TOKENS, turns * HEAD_SIZE)
    return pl.pallas_call(
        functools.partial(split_kernel, uly_count),
        out_shape=jax.ShapeDtypeStruct(queries.shape, dtype),
        in_specs=[smem, smem, smem, hbm, hbm, hbm],
        out_specs=hbm,
        scratch_shapes=[
            pltpu.VMEM(key_state_rows.shape, dtype),
            pltpu.VMEM(value_state_rows.shape, dtype),
            dma((2,)),
            dma((8,)),
            dma((8,)),
            dma((8,)),
            dma((4,)),
            dma((4,)),
            dma((4,)),
            dma((8, length, 5)),
            dma((8, length, 2)),
            dma((8, length, 2)),
            dma((4, turns // GANG)),
            dma((4, turns // GANG)),
            dma((4, turns // GANG)),
        ]
        + [pltpu.VMEM((blocks, BLOCK_TOKENS, HEAD_SIZE), dtype)] * 8
        + [pltpu.VMEM(share, dtype)] * 16,
        compiler_params=pltpu.CompilerParams(collective_id=0, has_side_effects=True),
        name="split_and_attend",
    )(
        jnp.asarray(place_table(group_count, uly_count)),
        vert_blocks.T,
        slash_offsets.T,
        queries,
        key_state_rows,
        value_state_rows,
    )


def chosen(queries, key_state_rows, *rest):
    group_count, uly_count = lax.axis_size("grp"), lax.axis_size("uly")
    fits = (
        group_count == 4
        and uly_count == 8
        and KEY_VALUE_HEADS == 4 * HALVES
        and queries.shape[0] == BLOCK_TOKENS
    )
    plan = split_shards if fits else shards
    return plan(queries, key_state_rows, *rest)


def solution(mesh):
    return jax.shard_map(
        chosen,
        mesh=mesh,
        in_specs=(
            P(("grp", "uly"), None),
            P(("grp", "uly"), None),
            P(("grp", "uly"), None),
            P(),
            P(),
        ),
        out_specs=P(("grp", "uly"), None),
        check_vma=False,
    )
```

```python
import functools

import jax
import jax.numpy as jnp
import numpy as np
from jax import lax
from jax.experimental import pallas as pl
from jax.experimental.pallas import tpu as pltpu
from jax.sharding import PartitionSpec as P

QUERY_HEADS = 64
KEY_VALUE_HEADS = 8
HEAD_SIZE = 128
BLOCK_TOKENS = 128


neg_large = -1e30


def passed_along(value, axis, steps):
    count = lax.axis_size(axis)
    initial, last = (max(0, -steps), min(count, count - steps))
    return lax.ppermute(value, axis, [(source, source + steps) for source in range(initial, last)])


def add_slot(running, slot_scores, allowed, weigh):
    best, total, accum = running
    slot_scores = jnp.where(allowed, slot_scores, neg_large)
    new_best = jnp.maximum(best, jnp.max(slot_scores, axis=-1))
    factor = jnp.exp(best - new_best)
    weights = jnp.where(allowed, jnp.exp(slot_scores - new_best[..., None]), 0.0)
    total = total * factor + jnp.sum(weights, axis=-1)
    accum = accum * factor[..., None] + weigh(weights.astype(jnp.bfloat16))
    return (new_best, total, accum)


def shards(queries, key_state_rows, value_state_rows, vert_blocks, slash_offsets):
    ulysses_count = lax.axis_size("uly")
    group_id = lax.axis_index("grp")
    uly_id = lax.axis_index("uly")
    per_device = QUERY_HEADS // ulysses_count
    group_width = QUERY_HEADS // KEY_VALUE_HEADS
    token_rows = queries.shape[0]
    ordering = jnp.arange(QUERY_HEADS, dtype=jnp.int32)
    heads_per_slot = np.arange(ulysses_count) * per_device // group_width
    key_outgoing = key_state_rows.reshape(token_rows, KEY_VALUE_HEADS, HEAD_SIZE)[
        :, heads_per_slot
    ].reshape(token_rows, ulysses_count * HEAD_SIZE)
    value_outgoing = value_state_rows.reshape(token_rows, KEY_VALUE_HEADS, HEAD_SIZE)[
        :, heads_per_slot
    ].reshape(token_rows, ulysses_count * HEAD_SIZE)
    q_group, k_group, v_group = (
        lax.all_to_all(queries, "uly", split_axis=1, concat_axis=0, tiled=True),
        lax.all_to_all(key_outgoing, "uly", split_axis=1, concat_axis=0, tiled=True),
        lax.all_to_all(value_outgoing, "uly", split_axis=1, concat_axis=0, tiled=True),
    )
    seg_rows = q_group.shape[0]
    block_count = seg_rows // BLOCK_TOKENS
    reach = block_count // 2
    q_tiles = q_group.reshape(block_count, BLOCK_TOKENS, per_device, HEAD_SIZE)
    key_block_tiles = k_group.reshape(block_count, BLOCK_TOKENS, HEAD_SIZE)
    value_block_tiles = v_group.reshape(block_count, BLOCK_TOKENS, HEAD_SIZE)
    prior_k, prior_v = passed_along(
        (key_block_tiles[block_count - reach :], value_block_tiles[block_count - reach :]), "grp", 1
    )
    k_wide = jnp.concatenate([prior_k, key_block_tiles], axis=0)
    v_wide = jnp.concatenate([prior_v, value_block_tiles], axis=0)
    heads_here = lax.dynamic_slice_in_dim(ordering, uly_id * per_device, per_device)
    vert_list = jnp.take(vert_blocks, heads_here, axis=0)
    offset_list = jnp.take(slash_offsets, heads_here, axis=0)
    local_block = jnp.where(vert_list >= 0, vert_list % block_count, 0)
    owned = (vert_list >= 0) & (vert_list // block_count == group_id)
    pick_k = jnp.where(
        owned[:, :, None, None], key_block_tiles[local_block], jnp.zeros((), jnp.bfloat16)
    )
    pick_v = jnp.where(
        owned[:, :, None, None], value_block_tiles[local_block], jnp.zeros((), jnp.bfloat16)
    )
    summed_k, summed_v = (
        lax.psum(pick_k.astype(jnp.float32).astype(jnp.bfloat16), "grp").astype(jnp.float32),
        lax.psum(pick_v.astype(jnp.float32).astype(jnp.bfloat16), "grp").astype(jnp.float32),
    )
    vert_k = summed_k.astype(jnp.bfloat16)
    vert_v = summed_v.astype(jnp.bfloat16)
    query_blocks = group_id * block_count + jnp.arange(block_count, dtype=jnp.int32)
    score_scale = HEAD_SIZE ** (-0.5)
    causal = (jnp.arange(BLOCK_TOKENS)[:, None] >= jnp.arange(BLOCK_TOKENS)[None, :])[
        None, :, None, :
    ]
    diag_scores = (
        jnp.einsum("nqhd,nkd->nqhk", q_tiles, key_block_tiles, preferred_element_type=jnp.float32)
        * score_scale
    )
    diag_scores = jnp.where(causal, diag_scores, neg_large)
    best = jnp.max(diag_scores, axis=-1)
    diag_weights = jnp.where(causal, jnp.exp(diag_scores - best[..., None]), 0.0)
    total = jnp.sum(diag_weights, axis=-1)
    accum = jnp.einsum(
        "nqhk,nkd->nqhd",
        diag_weights.astype(jnp.bfloat16),
        value_block_tiles,
        preferred_element_type=jnp.float32,
    )
    running = (best, total, accum)

    def slash_slot(slot_index, running):
        offset_now = lax.dynamic_index_in_dim(offset_list, slot_index, axis=1, keepdims=False)
        starts = jnp.where(offset_now >= 1, reach - offset_now, 0)

        def near_slice(begin_at):
            return (
                lax.dynamic_slice_in_dim(k_wide, begin_at, block_count, 0),
                lax.dynamic_slice_in_dim(v_wide, begin_at, block_count, 0),
            )

        k_near, v_near = jax.vmap(near_slice)(starts)
        allowed = (offset_now[None, :] >= 1) & (query_blocks[:, None] - offset_now[None, :] >= 0)
        slot_scores = (
            jnp.einsum("nqhd,hnkd->nqhk", q_tiles, k_near, preferred_element_type=jnp.float32)
            * score_scale
        )

        def weigh_near(prob_low):
            return jnp.einsum(
                "nqhk,hnkd->nqhd", prob_low, v_near, preferred_element_type=jnp.float32
            )

        return add_slot(running, slot_scores, allowed[:, None, :, None], weigh_near)

    slash_turns = jnp.max(jnp.sum((offset_list >= 1).astype(jnp.int32), axis=1))
    running = lax.fori_loop(0, slash_turns, slash_slot, running)

    def vert_slot(slot_index, running):
        block_now = lax.dynamic_index_in_dim(vert_list, slot_index, axis=1, keepdims=False)
        k_far = lax.dynamic_index_in_dim(vert_k, slot_index, axis=1, keepdims=False)
        v_far = lax.dynamic_index_in_dim(vert_v, slot_index, axis=1, keepdims=False)
        hits = (offset_list[None, :, :] >= 1) & (
            query_blocks[:, None, None] - offset_list[None, :, :] == block_now[None, :, None]
        )
        allowed = (
            (block_now[None, :] >= 0)
            & (block_now[None, :] < query_blocks[:, None])
            & jnp.logical_not(jnp.any(hits, axis=2))
        )
        slot_scores = (
            jnp.einsum("nqhd,hkd->nqhk", q_tiles, k_far, preferred_element_type=jnp.float32)
            * score_scale
        )

        def weigh_far(prob_low):
            return jnp.einsum("nqhk,hkd->nqhd", prob_low, v_far, preferred_element_type=jnp.float32)

        return add_slot(running, slot_scores, allowed[:, None, :, None], weigh_far)

    vert_turns = jnp.max(jnp.sum((vert_list >= 0).astype(jnp.int32), axis=1))
    best, total, accum = lax.fori_loop(0, vert_turns, vert_slot, running)
    mixed = (
        (accum / total[..., None]).astype(jnp.bfloat16).reshape(seg_rows, per_device * HEAD_SIZE)
    )
    returned = lax.all_to_all(mixed, "uly", split_axis=0, concat_axis=1, tiled=True)
    return returned


MESH = pl.DeviceIdType.MESH
LOG2_E = 1.4426950408889634
HALVES = 2
PHASES = ((1, 0), (0, 0), (1, 1), (0, 1))
UP, DOWN, ACROSS, BESIDE, UP_TOO, DOWN_TOO, BESIDE_TOO = range(7)
WIDE_FIRST = ()
EAGER = True
GANG = 2


def axis_pair(half):
    return ("y", "x") if half == 0 else ("x", "y")


def whereabouts(group, member):
    return {"x": group // 2, "core": group % 2, "y": member % 2, "z": member // 2}


def flipped(where, axis):
    return {**where, axis: 1 - where[axis]}


def place_of(half, where, length):
    shared, other = axis_pair(half)
    return ((where["core"] * length + where["z"]) * 2 + where[other]) * 2 + where[shared]


def place_table(group_count, uly_count):
    block = np.arange(group_count * uly_count)
    where = whereabouts(block // uly_count, block % uly_count)
    rows = [place_of(half, where, uly_count // 2) for half in range(HALVES)]
    return np.stack(rows).astype(np.int32)


def attend(row, units, k_buf, v_buf, place_ref, vert_ref, slash_ref):
    slash_slots, vert_slots = slash_ref.shape[0], vert_ref.shape[0]
    rate = HEAD_SIZE ** (-0.5) * LOG2_E
    causal = lax.broadcasted_iota(
        jnp.int32, (BLOCK_TOKENS, BLOCK_TOKENS), 0
    ) >= lax.broadcasted_iota(jnp.int32, (BLOCK_TOKENS, BLOCK_TOKENS), 1)

    def slots_of(q_head, here):
        blocks, allowed = [here], [None]
        offsets = [slash_ref[slot, q_head] for slot in range(slash_slots)]
        for offset in offsets:
            ok = (offset >= 1) & (here - offset >= 0)
            blocks.append(jnp.where(ok, here - offset, here))
            allowed.append(ok)
        for slot in range(vert_slots):
            block = vert_ref[slot, q_head]
            ok = (block >= 0) & (block < here)
            for offset in offsets:
                ok = ok & jnp.logical_not((offset >= 1) & (here - offset == block))
            blocks.append(jnp.where(ok, block, here))
            allowed.append(ok)
        return blocks, allowed

    chosen_slots = [slots_of(q_head, here) for _, _, _, q_head, here in units]
    scores, probs, totals = [], [], []
    for (q_ref, _, columns, _, _), (blocks, _) in zip(units, chosen_slots):
        keys = jnp.concatenate([k_buf[place_ref[row, block]] for block in blocks], axis=0)
        scores.append(
            lax.dot_general(
                q_ref[:, columns],
                keys,
                (((1,), (1,)), ((), ())),
                preferred_element_type=jnp.float32,
            )
        )
    for score, (_, allowed) in zip(scores, chosen_slots):
        pieces = []
        for slot, ok in enumerate(allowed):
            piece = score[:, slot * BLOCK_TOKENS : (slot + 1) * BLOCK_TOKENS]
            if ok is None:
                pieces.append(jnp.where(causal, piece, neg_large))
            else:
                pieces.append(piece + jnp.where(ok, 0.0, neg_large).astype(jnp.float32))
        best = functools.reduce(jnp.maximum, pieces)
        best = jnp.max(best, axis=1, keepdims=True)
        weights = [jnp.exp2((piece - best) * rate) for piece in pieces]
        total = functools.reduce(jnp.add, weights)
        totals.append(jnp.sum(total, axis=1, keepdims=True))
        probs.append(jnp.concatenate([weight.astype(jnp.bfloat16) for weight in weights], axis=1))
    for (_, o_ref, columns, _, _), prob, total, (blocks, _) in zip(
        units, probs, totals, chosen_slots
    ):
        values = jnp.concatenate([v_buf[place_ref[row, block]] for block in blocks], axis=0)
        mixed = jnp.dot(prob, values, preferred_element_type=jnp.float32)
        o_ref[:, columns] = (mixed / total).astype(o_ref.dtype)


def split_kernel(
    uly_count,
    place_ref,
    vert_ref,
    slash_ref,
    q_hbm,
    k_hbm,
    v_hbm,
    out_ref,
    k_own,
    v_own,
    load_sem,
    own_sem,
    ex_send,
    ex_recv,
    q_sem,
    q_send,
    q_recv,
    g_send,
    g_recv,
    b_recv,
    o_sem,
    o_send,
    o_recv,
    *buffers,
):
    length = uly_count // 2
    group, member = lax.axis_index("grp"), lax.axis_index("uly")
    me = whereabouts(group, member)
    z = me["z"]
    per_kv = q_hbm.shape[1] // KEY_VALUE_HEADS
    turns = per_kv // HEAD_SIZE
    gangs = turns // GANG
    held = buffers[:8]
    q_bufs = [buffers[8 + 2 * n : 10 + 2 * n] for n in range(4)]
    o_bufs = [buffers[16 + 2 * n : 18 + 2 * n] for n in range(4)]
    sources = (k_own, v_own)

    def block_at(where):
        return (where["x"] * 2 + where["core"]) * uly_count + where["z"] * 2 + where["y"]

    def device_at(where):
        return (where["x"] * 2 + where["core"], where["z"] * 2 + where["y"])

    def partner(half):
        return flipped(me, axis_pair(half)[0])

    def kv_head(half, n, where):
        return (half * 2 + where[axis_pair(half)[0]]) * 2 + n

    def lanes(start, width):
        return pl.ds(pl.multiple_of(start, HEAD_SIZE), width)

    loads = []
    for n, (source, target) in enumerate(((k_hbm, k_own), (v_hbm, v_own))):
        loads.append(pltpu.make_async_copy(source, target, load_sem.at[n]))
        loads[-1].start()
    own, q_own = {}, {}
    for half, n in PHASES:
        for kind, source in enumerate((k_hbm, v_hbm)):
            item = (half * 2 + n) * 2 + kind
            columns = lanes(kv_head(half, n, me) * HEAD_SIZE, HEAD_SIZE)
            own[item] = pltpu.make_async_copy(
                source.at[:, columns], held[item].at[place_of(half, me, length)], own_sem.at[item]
            )
            own[item].start()
    for half, n in PHASES:
        columns = lanes(kv_head(half, n, me) * per_kv, per_kv)
        q_own[half, n] = pltpu.make_async_copy(
            q_hbm.at[:, columns], q_bufs[half * 2 + n][0], q_sem.at[half * 2 + n]
        )
        q_own[half, n].start()

    barrier = pltpu.get_barrier_semaphore()
    around = [flipped(me, axis) for axis in ("x", "y", "core")]
    for where in around:
        pl.semaphore_signal(barrier, inc=1, device_id=device_at(where), device_id_type=MESH)

    def greet(step):
        pl.semaphore_signal(
            barrier, inc=1, device_id=device_at({**me, "z": z + step}), device_id_type=MESH
        )

    pl.when(z > 0)(lambda: greet(-1))
    pl.when(z < length - 1)(lambda: greet(1))
    count = len(around) + jnp.where(z > 0, 1, 0) + jnp.where(z < length - 1, 1, 0)
    pl.semaphore_wait(barrier, count)
    for load in loads:
        load.wait()

    def remote(source, target, send, recv, where):
        return pltpu.make_async_remote_copy(
            src_ref=source,
            dst_ref=target,
            send_sem=send,
            recv_sem=recv,
            device_id=device_at(where),
            device_id_type=MESH,
        )

    sent = []

    def begin(copy):
        copy.start()
        sent.append(copy)
        return copy

    exchanged, asked, answered, own_out = {}, {}, [], []

    def exchange(half, n):
        peer = partner(half)
        columns = lanes(kv_head(half, n, peer) * HEAD_SIZE, HEAD_SIZE)
        for kind in range(2):
            item = (half * 2 + n) * 2 + kind
            exchanged[item] = begin(
                remote(
                    sources[kind].at[:, columns],
                    held[item].at[place_of(half, me, length)],
                    ex_send.at[item],
                    ex_recv.at[item],
                    peer,
                )
            )

    def ask(half, n):
        peer = partner(half)
        columns = lanes(kv_head(half, n, peer) * per_kv, per_kv)
        asked[half, n] = begin(
            remote(
                q_hbm.at[:, columns],
                q_bufs[half * 2 + n][1],
                q_send.at[half * 2 + n],
                q_recv.at[half * 2 + n],
                peer,
            )
        )

    def part_of(item, core, slab, lane):
        other = axis_pair(item // 4)[1]
        side = me[other] if lane == 0 else 1 - me[other]
        return held[item].at[pl.ds(((core * length + slab) * 2 + side) * 2, 2)]

    def hop(item, slab, way, part=None):
        other = axis_pair(item // 4)[1]
        lane = 1 if way in (UP_TOO, DOWN_TOO, BESIDE_TOO) else 0
        if part is None:
            part = part_of(item, me["core"], slab, lane)
        if way in (BESIDE, BESIDE_TOO):
            where, recv = flipped(me, "core"), b_recv.at[item, slab, lane]
        elif way == ACROSS:
            where, recv = flipped(me, other), g_recv.at[item, slab, 1]
        else:
            where = {**me, "z": z + (1 if way in (UP, UP_TOO) else -1)}
            recv = g_recv.at[item, slab, lane]
        return remote(part, part, g_send.at[item, slab, way], recv, where)

    def wait_for(item, slab, lane):
        part = part_of(item, me["core"], slab, lane)
        recv = g_recv.at[item, slab, lane]
        remote(part, part, g_send.at[item, slab, 0], recv, me).wait_recv()

    def wait_beside(item, slab, lane):
        part = part_of(item, 1 - me["core"], slab, lane)
        recv = b_recv.at[item, slab, lane]
        remote(part, part, g_send.at[item, slab, 0], recv, me).wait_recv()

    def each_way(item, slab, ways, act, part=None):
        for way in ways:
            if way in (UP, UP_TOO):
                ok = z < length - 1
            elif way in (DOWN, DOWN_TOO):
                ok = z > 0
            elif way == ACROSS and item < 4:
                ok = me["x"] == 0
            else:
                ok = None
            if ok is None:
                act(hop(item, slab, way, part))
            else:
                pl.when(ok)(lambda way=way: act(hop(item, slab, way, part)))

    def started(copy):
        copy.start()

    def finished(copy):
        copy.wait_send()

    def visit(item, distance, act, wait=False):
        first = item in WIDE_FIRST
        if distance == 0:
            each_way(item, z, (UP, DOWN, ACROSS, BESIDE), act)
            return
        across = () if first else (ACROSS,)

        @pl.when(z >= distance)
        def _():
            if wait:
                wait_for(item, z - distance, 0)
            each_way(item, z - distance, (UP,) + across + (BESIDE,), act)

        @pl.when(z + distance < length)
        def _():
            if wait:
                wait_for(item, z + distance, 0)
            each_way(item, z + distance, (DOWN,) + across + (BESIDE,), act)

        if first:
            visit_too(item, distance, act, wait)

    def visit_too(item, distance, act, wait=False):
        @crossed(item)
        def _():
            if distance == 0:
                if wait:
                    wait_for(item, z, 1)
                each_way(item, z, (UP_TOO, DOWN_TOO, BESIDE_TOO), act)
                return

            @pl.when(z >= distance)
            def _():
                if wait:
                    wait_for(item, z - distance, 1)
                each_way(item, z - distance, (UP_TOO, BESIDE_TOO), act)

            @pl.when(z + distance < length)
            def _():
                if wait:
                    wait_for(item, z + distance, 1)
                each_way(item, z + distance, (DOWN_TOO, BESIDE_TOO), act)

    def crossed(item):
        return lambda body: body() if item >= 4 else pl.when(me["x"] == 1)(body)

    def items_of(phase):
        half, n = PHASES[phase]
        return [(half * 2 + n) * 2 + kind for kind in range(2)]

    def launch(item):
        own[item].wait()
        exchanged[item].wait_recv()
        visit(item, 0, started)

    def launch_early(item, mine):
        half = item // 4
        where = me if mine else partner(half)
        if mine:
            own[item].wait()
        else:
            exchanged[item].wait_recv()
        block = held[item].at[pl.ds(place_of(half, where, length), 1)]
        each_way(item, z, (UP, DOWN, ACROSS, BESIDE), started, block)

    def step(item, distance):
        if distance == 0:
            launch(item)
        elif distance == "too":
            visit_too(item, 0, started, wait=True)
        else:
            visit(item, distance, started, wait=True)

    def steps(phase, distance):
        todo = [(item, distance) for item in items_of(phase)]
        if distance == 0:
            todo += [(item, "too") for item in items_of(phase) if item in WIDE_FIRST]
        return todo

    def settle(phase):
        for item in items_of(phase):
            @crossed(item)
            def _():
                if item in WIDE_FIRST:
                    return
                for slab in range(length):
                    wait_for(item, slab, 1)
                    each_way(item, slab, (BESIDE_TOO,), started)

        for item in items_of(phase):
            for slab in range(length):
                wait_beside(item, slab, 0)

            @crossed(item)
            def _():
                for slab in range(length):
                    wait_beside(item, slab, 1)

        q_own[PHASES[phase]].wait()
        asked[PHASES[phase]].wait_recv()

    def drain(item):
        for distance in range(length):
            visit(item, distance, finished)

        if item in WIDE_FIRST:
            visit_too(item, 0, finished)
            return

        @crossed(item)
        def _():
            for slab in range(length):
                each_way(item, slab, (BESIDE_TOO,), finished)

    def answer(phase, gang):
        half, n = PHASES[phase]
        index = half * 2 + n
        width = GANG * HEAD_SIZE
        columns = lanes(kv_head(half, n, me) * per_kv + gang * width, width)
        local = pl.ds(gang * width, width)
        copy = begin(
            remote(
                o_bufs[index][1].at[:, local],
                out_ref.at[:, columns],
                o_send.at[index, gang],
                o_recv.at[index, gang],
                partner(half),
            )
        )
        answered.append(copy)
        copy = pltpu.make_async_copy(
            o_bufs[index][0].at[:, local], out_ref.at[:, columns], o_sem.at[index, gang]
        )
        copy.start()
        own_out.append(copy)

    def compute(phase, gang):
        half, n = PHASES[phase]
        index = half * 2 + n
        units = []
        for turn in range(gang * GANG, (gang + 1) * GANG):
            for side, where in enumerate((me, partner(half))):
                units.append(
                    (
                        q_bufs[index][side],
                        o_bufs[index][side],
                        pl.ds(turn * HEAD_SIZE, HEAD_SIZE),
                        kv_head(half, n, me) * turns + turn,
                        block_at(where),
                    )
                )
        k_item, v_item = items_of(phase)
        attend(half, units, held[k_item], held[v_item], place_ref, vert_ref, slash_ref)

    def run(todo):
        for item, distance in todo:
            step(item, distance)

    for phase in range(4):
        exchange(*PHASES[phase])
    ask(*PHASES[0])
    ask(*PHASES[2])
    if EAGER:
        for mine in (True, False):
            for item in items_of(0):
                launch_early(item, mine)
        run(steps(0, 0)[2:] + steps(0, 1))
    else:
        run(steps(0, 0) + steps(0, 1))
    run(steps(1, 0) + steps(0, 2) + steps(1, 1) + steps(0, 3))
    ask(*PHASES[1])
    run(steps(2, 0) + steps(1, 2) + steps(2, 1) + steps(1, 3))
    later = [
        steps(3, 0) + steps(2, 2) + steps(3, 1)[:1],
        steps(3, 1)[1:] + steps(2, 3) + steps(3, 2)[:1],
        steps(3, 2)[1:] + steps(3, 3),
    ]
    for phase in range(4):
        settle(phase)
        todo = later[phase] if phase < 3 else []
        if phase == 2:
            ask(*PHASES[3])
        for gang in range(gangs):
            compute(phase, gang)
            share = -(-len(todo) // (gangs - gang))
            run(todo[:share])
            todo = todo[share:]
            if phase != 2:
                answer(phase, gang)
        if phase == 2:
            for gang in range(gangs):
                answer(phase, gang)
    for copy in sent:
        copy.wait_send()
    for item in range(8):
        drain(item)
    for copy in answered:
        copy.wait_recv()
    for copy in own_out:
        copy.wait()


def split_shards(queries, key_state_rows, value_state_rows, vert_blocks, slash_offsets):
    group_count, uly_count = lax.axis_size("grp"), lax.axis_size("uly")
    blocks = group_count * uly_count
    length = uly_count // 2
    turns = QUERY_HEADS // KEY_VALUE_HEADS
    dtype = queries.dtype
    smem = pl.BlockSpec(memory_space=pltpu.SMEM)
    hbm = pl.BlockSpec(memory_space=pl.ANY)
    dma = pltpu.SemaphoreType.DMA
    share = (BLOCK_TOKENS, turns * HEAD_SIZE)
    return pl.pallas_call(
        functools.partial(split_kernel, uly_count),
        out_shape=pltpu.VMEM(queries.shape, dtype),
        in_specs=[smem, smem, smem, hbm, hbm, hbm],
        out_specs=pl.BlockSpec(memory_space=pltpu.VMEM),
        scratch_shapes=[
            pltpu.VMEM(key_state_rows.shape, dtype),
            pltpu.VMEM(value_state_rows.shape, dtype),
            dma((2,)),
            dma((8,)),
            dma((8,)),
            dma((8,)),
            dma((4,)),
            dma((4,)),
            dma((4,)),
            dma((8, length, 7)),
            dma((8, length, 2)),
            dma((8, length, 2)),
            dma((4, turns // GANG)),
            dma((4, turns // GANG)),
            dma((4, turns // GANG)),
        ]
        + [pltpu.VMEM((blocks, BLOCK_TOKENS, HEAD_SIZE), dtype)] * 8
        + [pltpu.VMEM(share, dtype)] * 16,
        compiler_params=pltpu.CompilerParams(collective_id=0, has_side_effects=True),
        name="split_and_attend",
    )(
        jnp.asarray(place_table(group_count, uly_count)),
        vert_blocks.T,
        slash_offsets.T,
        queries,
        key_state_rows,
        value_state_rows,
    )


def chosen(queries, key_state_rows, *rest):
    group_count, uly_count = lax.axis_size("grp"), lax.axis_size("uly")
    fits = (
        group_count == 4
        and uly_count == 8
        and KEY_VALUE_HEADS == 4 * HALVES
        and queries.shape[0] == BLOCK_TOKENS
    )
    plan = split_shards if fits else shards
    return plan(queries, key_state_rows, *rest)


def solution(mesh):
    return jax.shard_map(
        chosen,
        mesh=mesh,
        in_specs=(
            P(("grp", "uly"), None),
            P(("grp", "uly"), None),
            P(("grp", "uly"), None),
            P(),
            P(),
        ),
        out_specs=P(("grp", "uly"), None),
        check_vma=False,
    )
```

```python
import functools

import jax
import jax.numpy as jnp
import numpy as np
from jax import lax
from jax.experimental import pallas as pl
from jax.experimental.pallas import tpu as pltpu
from jax.sharding import PartitionSpec as P

QUERY_HEADS = 64
KEY_VALUE_HEADS = 8
HEAD_SIZE = 128
BLOCK_TOKENS = 128


neg_large = -1e30


def passed_along(value, axis, steps):
    count = lax.axis_size(axis)
    initial, last = (max(0, -steps), min(count, count - steps))
    return lax.ppermute(value, axis, [(source, source + steps) for source in range(initial, last)])


def add_slot(running, slot_scores, allowed, weigh):
    best, total, accum = running
    slot_scores = jnp.where(allowed, slot_scores, neg_large)
    new_best = jnp.maximum(best, jnp.max(slot_scores, axis=-1))
    factor = jnp.exp(best - new_best)
    weights = jnp.where(allowed, jnp.exp(slot_scores - new_best[..., None]), 0.0)
    total = total * factor + jnp.sum(weights, axis=-1)
    accum = accum * factor[..., None] + weigh(weights.astype(jnp.bfloat16))
    return (new_best, total, accum)


def shards(queries, key_state_rows, value_state_rows, vert_blocks, slash_offsets):
    ulysses_count = lax.axis_size("uly")
    group_id = lax.axis_index("grp")
    uly_id = lax.axis_index("uly")
    per_device = QUERY_HEADS // ulysses_count
    group_width = QUERY_HEADS // KEY_VALUE_HEADS
    token_rows = queries.shape[0]
    ordering = jnp.arange(QUERY_HEADS, dtype=jnp.int32)
    heads_per_slot = np.arange(ulysses_count) * per_device // group_width
    key_outgoing = key_state_rows.reshape(token_rows, KEY_VALUE_HEADS, HEAD_SIZE)[
        :, heads_per_slot
    ].reshape(token_rows, ulysses_count * HEAD_SIZE)
    value_outgoing = value_state_rows.reshape(token_rows, KEY_VALUE_HEADS, HEAD_SIZE)[
        :, heads_per_slot
    ].reshape(token_rows, ulysses_count * HEAD_SIZE)
    q_group, k_group, v_group = (
        lax.all_to_all(queries, "uly", split_axis=1, concat_axis=0, tiled=True),
        lax.all_to_all(key_outgoing, "uly", split_axis=1, concat_axis=0, tiled=True),
        lax.all_to_all(value_outgoing, "uly", split_axis=1, concat_axis=0, tiled=True),
    )
    seg_rows = q_group.shape[0]
    block_count = seg_rows // BLOCK_TOKENS
    reach = block_count // 2
    q_tiles = q_group.reshape(block_count, BLOCK_TOKENS, per_device, HEAD_SIZE)
    key_block_tiles = k_group.reshape(block_count, BLOCK_TOKENS, HEAD_SIZE)
    value_block_tiles = v_group.reshape(block_count, BLOCK_TOKENS, HEAD_SIZE)
    prior_k, prior_v = passed_along(
        (key_block_tiles[block_count - reach :], value_block_tiles[block_count - reach :]), "grp", 1
    )
    k_wide = jnp.concatenate([prior_k, key_block_tiles], axis=0)
    v_wide = jnp.concatenate([prior_v, value_block_tiles], axis=0)
    heads_here = lax.dynamic_slice_in_dim(ordering, uly_id * per_device, per_device)
    vert_list = jnp.take(vert_blocks, heads_here, axis=0)
    offset_list = jnp.take(slash_offsets, heads_here, axis=0)
    local_block = jnp.where(vert_list >= 0, vert_list % block_count, 0)
    owned = (vert_list >= 0) & (vert_list // block_count == group_id)
    pick_k = jnp.where(
        owned[:, :, None, None], key_block_tiles[local_block], jnp.zeros((), jnp.bfloat16)
    )
    pick_v = jnp.where(
        owned[:, :, None, None], value_block_tiles[local_block], jnp.zeros((), jnp.bfloat16)
    )
    summed_k, summed_v = (
        lax.psum(pick_k.astype(jnp.float32).astype(jnp.bfloat16), "grp").astype(jnp.float32),
        lax.psum(pick_v.astype(jnp.float32).astype(jnp.bfloat16), "grp").astype(jnp.float32),
    )
    vert_k = summed_k.astype(jnp.bfloat16)
    vert_v = summed_v.astype(jnp.bfloat16)
    query_blocks = group_id * block_count + jnp.arange(block_count, dtype=jnp.int32)
    score_scale = HEAD_SIZE ** (-0.5)
    causal = (jnp.arange(BLOCK_TOKENS)[:, None] >= jnp.arange(BLOCK_TOKENS)[None, :])[
        None, :, None, :
    ]
    diag_scores = (
        jnp.einsum("nqhd,nkd->nqhk", q_tiles, key_block_tiles, preferred_element_type=jnp.float32)
        * score_scale
    )
    diag_scores = jnp.where(causal, diag_scores, neg_large)
    best = jnp.max(diag_scores, axis=-1)
    diag_weights = jnp.where(causal, jnp.exp(diag_scores - best[..., None]), 0.0)
    total = jnp.sum(diag_weights, axis=-1)
    accum = jnp.einsum(
        "nqhk,nkd->nqhd",
        diag_weights.astype(jnp.bfloat16),
        value_block_tiles,
        preferred_element_type=jnp.float32,
    )
    running = (best, total, accum)

    def slash_slot(slot_index, running):
        offset_now = lax.dynamic_index_in_dim(offset_list, slot_index, axis=1, keepdims=False)
        starts = jnp.where(offset_now >= 1, reach - offset_now, 0)

        def near_slice(begin_at):
            return (
                lax.dynamic_slice_in_dim(k_wide, begin_at, block_count, 0),
                lax.dynamic_slice_in_dim(v_wide, begin_at, block_count, 0),
            )

        k_near, v_near = jax.vmap(near_slice)(starts)
        allowed = (offset_now[None, :] >= 1) & (query_blocks[:, None] - offset_now[None, :] >= 0)
        slot_scores = (
            jnp.einsum("nqhd,hnkd->nqhk", q_tiles, k_near, preferred_element_type=jnp.float32)
            * score_scale
        )

        def weigh_near(prob_low):
            return jnp.einsum(
                "nqhk,hnkd->nqhd", prob_low, v_near, preferred_element_type=jnp.float32
            )

        return add_slot(running, slot_scores, allowed[:, None, :, None], weigh_near)

    slash_turns = jnp.max(jnp.sum((offset_list >= 1).astype(jnp.int32), axis=1))
    running = lax.fori_loop(0, slash_turns, slash_slot, running)

    def vert_slot(slot_index, running):
        block_now = lax.dynamic_index_in_dim(vert_list, slot_index, axis=1, keepdims=False)
        k_far = lax.dynamic_index_in_dim(vert_k, slot_index, axis=1, keepdims=False)
        v_far = lax.dynamic_index_in_dim(vert_v, slot_index, axis=1, keepdims=False)
        hits = (offset_list[None, :, :] >= 1) & (
            query_blocks[:, None, None] - offset_list[None, :, :] == block_now[None, :, None]
        )
        allowed = (
            (block_now[None, :] >= 0)
            & (block_now[None, :] < query_blocks[:, None])
            & jnp.logical_not(jnp.any(hits, axis=2))
        )
        slot_scores = (
            jnp.einsum("nqhd,hkd->nqhk", q_tiles, k_far, preferred_element_type=jnp.float32)
            * score_scale
        )

        def weigh_far(prob_low):
            return jnp.einsum("nqhk,hkd->nqhd", prob_low, v_far, preferred_element_type=jnp.float32)

        return add_slot(running, slot_scores, allowed[:, None, :, None], weigh_far)

    vert_turns = jnp.max(jnp.sum((vert_list >= 0).astype(jnp.int32), axis=1))
    best, total, accum = lax.fori_loop(0, vert_turns, vert_slot, running)
    mixed = (
        (accum / total[..., None]).astype(jnp.bfloat16).reshape(seg_rows, per_device * HEAD_SIZE)
    )
    returned = lax.all_to_all(mixed, "uly", split_axis=0, concat_axis=1, tiled=True)
    return returned


MESH = pl.DeviceIdType.MESH
LOG2_E = 1.4426950408889634
HALVES = 2
PHASES = ((1, 0), (0, 0), (1, 1), (0, 1))
UP, DOWN, ACROSS, BESIDE, UP_TOO, DOWN_TOO, BESIDE_TOO = range(7)
SHORT = ()
GANG = 2


def axis_pair(half):
    return ("y", "x") if half == 0 else ("x", "y")


def whereabouts(group, member):
    return {"x": group // 2, "core": group % 2, "y": member % 2, "z": member // 2}


def flipped(where, axis):
    return {**where, axis: 1 - where[axis]}


def place_of(half, where, length):
    shared, other = axis_pair(half)
    return ((where["core"] * length + where["z"]) * 2 + where[other]) * 2 + where[shared]


def attend(units, k_buf, v_buf, table_ref, bias_ref):
    slots = range(table_ref.shape[1])
    rate = HEAD_SIZE ** (-0.5) * LOG2_E
    causal = lax.broadcasted_iota(
        jnp.int32, (BLOCK_TOKENS, BLOCK_TOKENS), 0
    ) >= lax.broadcasted_iota(jnp.int32, (BLOCK_TOKENS, BLOCK_TOKENS), 1)
    scores, probs, totals = [], [], []
    for q_ref, _, columns, line in units:
        keys = jnp.concatenate([k_buf[table_ref[line, slot]] for slot in slots], axis=0)
        scores.append(
            lax.dot_general(
                q_ref[:, columns],
                keys,
                (((1,), (1,)), ((), ())),
                preferred_element_type=jnp.float32,
            )
        )
    for score, (_, _, _, line) in zip(scores, units):
        pieces = []
        for slot in slots:
            piece = score[:, slot * BLOCK_TOKENS : (slot + 1) * BLOCK_TOKENS]
            if slot == 0:
                pieces.append(jnp.where(causal, piece, neg_large))
            else:
                pieces.append(piece + bias_ref[line, slot])
        best = functools.reduce(jnp.maximum, pieces)
        best = jnp.max(best, axis=1, keepdims=True)
        weights = [jnp.exp2((piece - best) * rate) for piece in pieces]
        total = functools.reduce(jnp.add, weights)
        totals.append(jnp.sum(total, axis=1, keepdims=True))
        probs.append(jnp.concatenate([weight.astype(jnp.bfloat16) for weight in weights], axis=1))
    for (_, o_ref, columns, line), prob, total in zip(units, probs, totals):
        values = jnp.concatenate([v_buf[table_ref[line, slot]] for slot in slots], axis=0)
        mixed = jnp.dot(prob, values, preferred_element_type=jnp.float32)
        o_ref[:, columns] = (mixed / total).astype(o_ref.dtype)


def split_kernel(
    uly_count,
    vert_hbm,
    slash_hbm,
    q_hbm,
    k_hbm,
    v_hbm,
    out_ref,
    vert_ref,
    slash_ref,
    list_sem,
    table_ref,
    bias_ref,
    k_own,
    v_own,
    load_sem,
    own_sem,
    ex_send,
    ex_recv,
    q_sem,
    q_send,
    q_recv,
    g_send,
    g_recv,
    b_recv,
    o_sem,
    o_send,
    o_recv,
    *buffers,
):
    length = uly_count // 2
    group, member = lax.axis_index("grp"), lax.axis_index("uly")
    me = whereabouts(group, member)
    z = me["z"]
    per_kv = q_hbm.shape[1] // KEY_VALUE_HEADS
    turns = per_kv // HEAD_SIZE
    gangs = turns // GANG
    held = buffers[:8]
    q_bufs = [buffers[8 + 2 * n : 10 + 2 * n] for n in range(4)]
    o_bufs = [buffers[16 + 2 * n : 18 + 2 * n] for n in range(4)]
    sources = (k_own, v_own)

    def block_at(where):
        return (where["x"] * 2 + where["core"]) * uly_count + where["z"] * 2 + where["y"]

    def device_at(where):
        return (where["x"] * 2 + where["core"], where["z"] * 2 + where["y"])

    def partner(half):
        return flipped(me, axis_pair(half)[0])

    def kv_head(half, n, where):
        return (half * 2 + where[axis_pair(half)[0]]) * 2 + n

    def lanes(start, width):
        return pl.ds(pl.multiple_of(start, HEAD_SIZE), width)

    lists = []
    for n, (source, target) in enumerate(((vert_hbm, vert_ref), (slash_hbm, slash_ref))):
        lists.append(pltpu.make_async_copy(source, target, list_sem.at[n]))
        lists[-1].start()
    loads = []
    for n, (source, target) in enumerate(((k_hbm, k_own), (v_hbm, v_own))):
        loads.append(pltpu.make_async_copy(source, target, load_sem.at[n]))
        loads[-1].start()
    own, q_own = {}, {}
    for half, n in PHASES:
        for kind, source in enumerate((k_hbm, v_hbm)):
            item = (half * 2 + n) * 2 + kind
            columns = lanes(kv_head(half, n, me) * HEAD_SIZE, HEAD_SIZE)
            own[item] = pltpu.make_async_copy(
                source.at[:, columns], held[item].at[place_of(half, me, length)], own_sem.at[item]
            )
            own[item].start()
    for half, n in PHASES:
        columns = lanes(kv_head(half, n, me) * per_kv, per_kv)
        q_own[half, n] = pltpu.make_async_copy(
            q_hbm.at[:, columns], q_bufs[half * 2 + n][0], q_sem.at[half * 2 + n]
        )
        q_own[half, n].start()

    barrier = pltpu.get_barrier_semaphore()
    around = [flipped(me, axis) for axis in ("x", "y", "core")]
    for where in around:
        pl.semaphore_signal(barrier, inc=1, device_id=device_at(where), device_id_type=MESH)

    def greet(step):
        pl.semaphore_signal(
            barrier, inc=1, device_id=device_at({**me, "z": z + step}), device_id_type=MESH
        )

    pl.when(z > 0)(lambda: greet(-1))
    pl.when(z < length - 1)(lambda: greet(1))
    count = len(around) + jnp.where(z > 0, 1, 0) + jnp.where(z < length - 1, 1, 0)
    pl.semaphore_wait(barrier, count)
    for load in loads:
        load.wait()

    def remote(source, target, send, recv, where):
        return pltpu.make_async_remote_copy(
            src_ref=source,
            dst_ref=target,
            send_sem=send,
            recv_sem=recv,
            device_id=device_at(where),
            device_id_type=MESH,
        )

    sent = []

    def begin(copy):
        copy.start()
        sent.append(copy)
        return copy

    exchanged, asked, answered, own_out = {}, {}, [], []

    def exchange(half, n):
        peer = partner(half)
        columns = lanes(kv_head(half, n, peer) * HEAD_SIZE, HEAD_SIZE)
        for kind in range(2):
            item = (half * 2 + n) * 2 + kind
            exchanged[item] = begin(
                remote(
                    sources[kind].at[:, columns],
                    held[item].at[place_of(half, me, length)],
                    ex_send.at[item],
                    ex_recv.at[item],
                    peer,
                )
            )

    def ask(half, n):
        peer = partner(half)
        columns = lanes(kv_head(half, n, peer) * per_kv, per_kv)
        asked[half, n] = begin(
            remote(
                q_hbm.at[:, columns],
                q_bufs[half * 2 + n][1],
                q_send.at[half * 2 + n],
                q_recv.at[half * 2 + n],
                peer,
            )
        )

    def part_of(item, core, slab, lane):
        other = axis_pair(item // 4)[1]
        side = me[other] if lane == 0 else 1 - me[other]
        return held[item].at[pl.ds(((core * length + slab) * 2 + side) * 2, 2)]

    def hop(item, slab, way, part=None):
        other = axis_pair(item // 4)[1]
        lane = 1 if way in (UP_TOO, DOWN_TOO, BESIDE_TOO) else 0
        if part is None:
            part = part_of(item, me["core"], slab, lane)
        if way in (BESIDE, BESIDE_TOO):
            where, recv = flipped(me, "core"), b_recv.at[item, slab, lane]
        elif way == ACROSS:
            where, recv = flipped(me, other), g_recv.at[item, slab, 1]
        else:
            where = {**me, "z": z + (1 if way in (UP, UP_TOO) else -1)}
            recv = g_recv.at[item, slab, lane]
        return remote(part, part, g_send.at[item, slab, way], recv, where)

    def wait_for(item, slab, lane):
        part = part_of(item, me["core"], slab, lane)
        recv = g_recv.at[item, slab, lane]
        remote(part, part, g_send.at[item, slab, 0], recv, me).wait_recv()

    def wait_beside(item, slab, lane):
        part = part_of(item, 1 - me["core"], slab, lane)
        recv = b_recv.at[item, slab, lane]
        remote(part, part, g_send.at[item, slab, 0], recv, me).wait_recv()

    def each_way(item, slab, ways, act, part=None):
        for way in ways:
            if way in (UP, UP_TOO):
                ok = z < length - 1
            elif way in (DOWN, DOWN_TOO):
                ok = z > 0
            elif way == ACROSS and item < 4:
                ok = me["x"] == 0
            else:
                ok = None
            if ok is None:
                act(hop(item, slab, way, part))
            else:
                pl.when(ok)(lambda way=way: act(hop(item, slab, way, part)))

    def started(copy):
        copy.start()

    def finished(copy):
        copy.wait_send()

    def visit(item, distance, act, wait=False):
        if distance == 0:
            each_way(item, z, (UP, DOWN, ACROSS, BESIDE), act)
            return
        across = () if item in SHORT and distance == 1 else (ACROSS,)

        @pl.when(z >= distance)
        def _():
            if wait:
                wait_for(item, z - distance, 0)
            each_way(item, z - distance, (UP,) + across + (BESIDE,), act)

        @pl.when(z + distance < length)
        def _():
            if wait:
                wait_for(item, z + distance, 0)
            each_way(item, z + distance, (DOWN,) + across + (BESIDE,), act)

    def visit_too(item, distance, act, wait=False):
        ways = (UP_TOO, DOWN_TOO, BESIDE_TOO) if distance == 0 and item in SHORT else (BESIDE_TOO,)

        @crossed(item)
        def _():
            @pl.when(z >= distance)
            def _():
                if wait:
                    wait_for(item, z - distance, 1)
                each_way(item, z - distance, ways, act)

            if distance:
                @pl.when(z + distance < length)
                def _():
                    if wait:
                        wait_for(item, z + distance, 1)
                    each_way(item, z + distance, ways, act)

    def crossed(item):
        return lambda body: body() if item >= 4 else pl.when(me["x"] == 1)(body)

    def items_of(phase):
        half, n = PHASES[phase]
        return [(half * 2 + n) * 2 + kind for kind in range(2)]

    def launch(item):
        own[item].wait()
        exchanged[item].wait_recv()
        visit(item, 0, started)

    def launch_early(item, mine):
        half = item // 4
        where = me if mine else partner(half)
        if mine:
            own[item].wait()
        else:
            exchanged[item].wait_recv()
        block = held[item].at[pl.ds(place_of(half, where, length), 1)]
        each_way(item, z, (UP, DOWN, ACROSS, BESIDE), started, block)

    def step(item, distance):
        if distance == 0:
            launch(item)
        elif distance < 0:
            visit_too(item, -1 - distance, started, wait=True)
        else:
            visit(item, distance, started, wait=True)

    def steps(phase, distance):
        todo = [(item, distance) for item in items_of(phase)]
        short = [item for item in items_of(phase) if item in SHORT]
        if distance == 1:
            todo += [(item, -1) for item in short]
        if distance == length - 1:
            todo += [(item, -2) for item in short]
        return todo

    def settle(phase):
        for item in items_of(phase):
            for distance in range(2 if item in SHORT else 0, length):
                visit_too(item, distance, started, wait=True)
        for item in items_of(phase):
            for slab in range(length):
                wait_beside(item, slab, 0)

            @crossed(item)
            def _():
                for slab in range(length):
                    wait_beside(item, slab, 1)

        q_own[PHASES[phase]].wait()
        asked[PHASES[phase]].wait_recv()

    def drain(item):
        for distance in range(length):
            visit(item, distance, finished)
            visit_too(item, distance, finished)

    def answer(phase, gang):
        half, n = PHASES[phase]
        index = half * 2 + n
        width = GANG * HEAD_SIZE
        columns = lanes(kv_head(half, n, me) * per_kv + gang * width, width)
        local = pl.ds(gang * width, width)
        copy = begin(
            remote(
                o_bufs[index][1].at[:, local],
                out_ref.at[:, columns],
                o_send.at[index, gang],
                o_recv.at[index, gang],
                partner(half),
            )
        )
        answered.append(copy)
        copy = pltpu.make_async_copy(
            o_bufs[index][0].at[:, local], out_ref.at[:, columns], o_sem.at[index, gang]
        )
        copy.start()
        own_out.append(copy)

    def compute(phase, gang):
        half, n = PHASES[phase]
        index = half * 2 + n
        units = []
        for turn in range(gang * GANG, (gang + 1) * GANG):
            for side in range(2):
                units.append(
                    (
                        q_bufs[index][side],
                        o_bufs[index][side],
                        pl.ds(turn * HEAD_SIZE, HEAD_SIZE),
                        (phase * turns + turn) * 2 + side,
                    )
                )
        k_item, v_item = items_of(phase)
        attend(units, held[k_item], held[v_item], table_ref, bias_ref)

    def tabulate(phase):
        half, n = PHASES[phase]
        first = kv_head(half, n, me) * turns
        if phase == 0:
            for copy in lists:
                copy.wait()

        def place_at(block):
            group, member = lax.div(block, uly_count), lax.rem(block, uly_count)
            where = {
                "x": lax.div(group, 2),
                "core": lax.rem(group, 2),
                "y": lax.rem(member, 2),
                "z": lax.div(member, 2),
            }
            return place_of(half, where, length)

        @pl.loop(0, turns)
        def _(turn):
            q_head = first + turn
            offsets = [slash_ref[slot, q_head] for slot in range(slash_ref.shape[0])]
            listed = [vert_ref[slot, q_head] for slot in range(vert_ref.shape[0])]
            for side, where in enumerate((me, partner(half))):
                line = (phase * turns + turn) * 2 + side
                here = block_at(where)
                rows = [(here, None)]
                targets = []
                for offset in offsets:
                    ok = (offset >= 1) & (here - offset >= 0)
                    targets.append(jnp.where(ok, here - offset, -1))
                    rows.append((here - offset, ok))
                for block in listed:
                    ok = (block >= 0) & (block < here)
                    for target in targets:
                        ok = ok & (block != target)
                    rows.append((block, ok))
                for slot, (block, ok) in enumerate(rows):
                    if ok is None:
                        table_ref[line, slot] = place_at(block)
                    else:
                        table_ref[line, slot] = place_at(jnp.where(ok, block, here))
                        bias_ref[line, slot] = jnp.where(ok, 0.0, neg_large).astype(jnp.float32)

    def run(todo):
        for item, distance in todo:
            step(item, distance)

    for phase in range(4):
        exchange(*PHASES[phase])
    ask(*PHASES[0])
    for mine in (True, False):
        for item in items_of(0):
            launch_early(item, mine)
    tabulate(0)
    run(steps(0, 1) + steps(1, 0))
    tabulate(1)
    run(steps(0, 2))
    tabulate(2)
    run(steps(1, 1) + steps(0, 3))
    ask(*PHASES[1])
    tabulate(3)
    run(steps(2, 0) + steps(1, 2) + steps(2, 1) + steps(1, 3))
    ask(*PHASES[2])
    run(steps(3, 0))
    between = (
        ((), (), steps(2, 2)[:1], steps(2, 2)[1:]),
        (steps(3, 1)[:1], steps(3, 1)[1:], steps(2, 3)[:1], steps(2, 3)[1:] + steps(3, 2)),
        ((), steps(3, 3)[:1], steps(3, 3)[1:], ()),
        ((), (), (), ()),
    )
    held_back = {0: (0,), 1: (1,), 2: (2,)}
    for phase in range(4):
        settle(phase)
        for gang in range(gangs):
            compute(phase, gang)
            run(between[phase][gang])
            if phase == 3:
                answer(phase, gang)
        if phase == 1:
            ask(*PHASES[3])
        for ready in held_back.get(phase, ()):
            for gang in range(gangs):
                answer(ready, gang)
    for copy in sent:
        copy.wait_send()
    for item in range(8):
        drain(item)
    for copy in answered:
        copy.wait_recv()
    for copy in own_out:
        copy.wait()


def split_shards(queries, key_state_rows, value_state_rows, vert_blocks, slash_offsets):
    group_count, uly_count = lax.axis_size("grp"), lax.axis_size("uly")
    blocks = group_count * uly_count
    length = uly_count // 2
    turns = QUERY_HEADS // KEY_VALUE_HEADS
    slots = 1 + slash_offsets.shape[1] + vert_blocks.shape[1]
    dtype = queries.dtype
    hbm = pl.BlockSpec(memory_space=pl.ANY)
    dma = pltpu.SemaphoreType.DMA
    share = (BLOCK_TOKENS, turns * HEAD_SIZE)
    return pl.pallas_call(
        functools.partial(split_kernel, uly_count),
        out_shape=pltpu.VMEM(queries.shape, dtype),
        in_specs=[hbm] * 5,
        out_specs=pl.BlockSpec(memory_space=pltpu.VMEM),
        scratch_shapes=[
            pltpu.SMEM(vert_blocks.shape[::-1], jnp.int32),
            pltpu.SMEM(slash_offsets.shape[::-1], jnp.int32),
            dma((2,)),
            pltpu.SMEM((8 * turns, slots), jnp.int32),
            pltpu.SMEM((8 * turns, slots), jnp.float32),
            pltpu.VMEM(key_state_rows.shape, dtype),
            pltpu.VMEM(value_state_rows.shape, dtype),
            dma((2,)),
            dma((8,)),
            dma((8,)),
            dma((8,)),
            dma((4,)),
            dma((4,)),
            dma((4,)),
            dma((8, length, 7)),
            dma((8, length, 2)),
            dma((8, length, 2)),
            dma((4, turns // GANG)),
            dma((4, turns // GANG)),
            dma((4, turns // GANG)),
        ]
        + [pltpu.VMEM((blocks, BLOCK_TOKENS, HEAD_SIZE), dtype)] * 8
        + [pltpu.VMEM(share, dtype)] * 16,
        compiler_params=pltpu.CompilerParams(collective_id=0, has_side_effects=True),
        name="split_and_attend",
    )(
        vert_blocks.T,
        slash_offsets.T,
        queries,
        key_state_rows,
        value_state_rows,
    )


def chosen(queries, key_state_rows, *rest):
    group_count, uly_count = lax.axis_size("grp"), lax.axis_size("uly")
    fits = (
        group_count == 4
        and uly_count == 8
        and KEY_VALUE_HEADS == 4 * HALVES
        and queries.shape[0] == BLOCK_TOKENS
    )
    plan = split_shards if fits else shards
    return plan(queries, key_state_rows, *rest)


def solution(mesh):
    return jax.shard_map(
        chosen,
        mesh=mesh,
        in_specs=(
            P(("grp", "uly"), None),
            P(("grp", "uly"), None),
            P(("grp", "uly"), None),
            P(),
            P(),
        ),
        out_specs=P(("grp", "uly"), None),
        check_vma=False,
    )
```

```python
import functools

import jax
import jax.numpy as jnp
import numpy as np
from jax import lax
from jax.experimental import pallas as pl
from jax.experimental.pallas import tpu as pltpu
from jax.sharding import PartitionSpec as P

QUERY_HEADS = 64
KEY_VALUE_HEADS = 8
HEAD_SIZE = 128
BLOCK_TOKENS = 128


neg_large = -1e30


def passed_along(value, axis, steps):
    count = lax.axis_size(axis)
    initial, last = (max(0, -steps), min(count, count - steps))
    return lax.ppermute(value, axis, [(source, source + steps) for source in range(initial, last)])


def add_slot(running, slot_scores, allowed, weigh):
    best, total, accum = running
    slot_scores = jnp.where(allowed, slot_scores, neg_large)
    new_best = jnp.maximum(best, jnp.max(slot_scores, axis=-1))
    factor = jnp.exp(best - new_best)
    weights = jnp.where(allowed, jnp.exp(slot_scores - new_best[..., None]), 0.0)
    total = total * factor + jnp.sum(weights, axis=-1)
    accum = accum * factor[..., None] + weigh(weights.astype(jnp.bfloat16))
    return (new_best, total, accum)


def shards(queries, key_state_rows, value_state_rows, vert_blocks, slash_offsets):
    ulysses_count = lax.axis_size("uly")
    group_id = lax.axis_index("grp")
    uly_id = lax.axis_index("uly")
    per_device = QUERY_HEADS // ulysses_count
    group_width = QUERY_HEADS // KEY_VALUE_HEADS
    token_rows = queries.shape[0]
    ordering = jnp.arange(QUERY_HEADS, dtype=jnp.int32)
    heads_per_slot = np.arange(ulysses_count) * per_device // group_width
    key_outgoing = key_state_rows.reshape(token_rows, KEY_VALUE_HEADS, HEAD_SIZE)[
        :, heads_per_slot
    ].reshape(token_rows, ulysses_count * HEAD_SIZE)
    value_outgoing = value_state_rows.reshape(token_rows, KEY_VALUE_HEADS, HEAD_SIZE)[
        :, heads_per_slot
    ].reshape(token_rows, ulysses_count * HEAD_SIZE)
    q_group, k_group, v_group = (
        lax.all_to_all(queries, "uly", split_axis=1, concat_axis=0, tiled=True),
        lax.all_to_all(key_outgoing, "uly", split_axis=1, concat_axis=0, tiled=True),
        lax.all_to_all(value_outgoing, "uly", split_axis=1, concat_axis=0, tiled=True),
    )
    seg_rows = q_group.shape[0]
    block_count = seg_rows // BLOCK_TOKENS
    reach = block_count // 2
    q_tiles = q_group.reshape(block_count, BLOCK_TOKENS, per_device, HEAD_SIZE)
    key_block_tiles = k_group.reshape(block_count, BLOCK_TOKENS, HEAD_SIZE)
    value_block_tiles = v_group.reshape(block_count, BLOCK_TOKENS, HEAD_SIZE)
    prior_k, prior_v = passed_along(
        (key_block_tiles[block_count - reach :], value_block_tiles[block_count - reach :]), "grp", 1
    )
    k_wide = jnp.concatenate([prior_k, key_block_tiles], axis=0)
    v_wide = jnp.concatenate([prior_v, value_block_tiles], axis=0)
    heads_here = lax.dynamic_slice_in_dim(ordering, uly_id * per_device, per_device)
    vert_list = jnp.take(vert_blocks, heads_here, axis=0)
    offset_list = jnp.take(slash_offsets, heads_here, axis=0)
    local_block = jnp.where(vert_list >= 0, vert_list % block_count, 0)
    owned = (vert_list >= 0) & (vert_list // block_count == group_id)
    pick_k = jnp.where(
        owned[:, :, None, None], key_block_tiles[local_block], jnp.zeros((), jnp.bfloat16)
    )
    pick_v = jnp.where(
        owned[:, :, None, None], value_block_tiles[local_block], jnp.zeros((), jnp.bfloat16)
    )
    summed_k, summed_v = (
        lax.psum(pick_k.astype(jnp.float32).astype(jnp.bfloat16), "grp").astype(jnp.float32),
        lax.psum(pick_v.astype(jnp.float32).astype(jnp.bfloat16), "grp").astype(jnp.float32),
    )
    vert_k = summed_k.astype(jnp.bfloat16)
    vert_v = summed_v.astype(jnp.bfloat16)
    query_blocks = group_id * block_count + jnp.arange(block_count, dtype=jnp.int32)
    score_scale = HEAD_SIZE ** (-0.5)
    causal = (jnp.arange(BLOCK_TOKENS)[:, None] >= jnp.arange(BLOCK_TOKENS)[None, :])[
        None, :, None, :
    ]
    diag_scores = (
        jnp.einsum("nqhd,nkd->nqhk", q_tiles, key_block_tiles, preferred_element_type=jnp.float32)
        * score_scale
    )
    diag_scores = jnp.where(causal, diag_scores, neg_large)
    best = jnp.max(diag_scores, axis=-1)
    diag_weights = jnp.where(causal, jnp.exp(diag_scores - best[..., None]), 0.0)
    total = jnp.sum(diag_weights, axis=-1)
    accum = jnp.einsum(
        "nqhk,nkd->nqhd",
        diag_weights.astype(jnp.bfloat16),
        value_block_tiles,
        preferred_element_type=jnp.float32,
    )
    running = (best, total, accum)

    def slash_slot(slot_index, running):
        offset_now = lax.dynamic_index_in_dim(offset_list, slot_index, axis=1, keepdims=False)
        starts = jnp.where(offset_now >= 1, reach - offset_now, 0)

        def near_slice(begin_at):
            return (
                lax.dynamic_slice_in_dim(k_wide, begin_at, block_count, 0),
                lax.dynamic_slice_in_dim(v_wide, begin_at, block_count, 0),
            )

        k_near, v_near = jax.vmap(near_slice)(starts)
        allowed = (offset_now[None, :] >= 1) & (query_blocks[:, None] - offset_now[None, :] >= 0)
        slot_scores = (
            jnp.einsum("nqhd,hnkd->nqhk", q_tiles, k_near, preferred_element_type=jnp.float32)
            * score_scale
        )

        def weigh_near(prob_low):
            return jnp.einsum(
                "nqhk,hnkd->nqhd", prob_low, v_near, preferred_element_type=jnp.float32
            )

        return add_slot(running, slot_scores, allowed[:, None, :, None], weigh_near)

    slash_turns = jnp.max(jnp.sum((offset_list >= 1).astype(jnp.int32), axis=1))
    running = lax.fori_loop(0, slash_turns, slash_slot, running)

    def vert_slot(slot_index, running):
        block_now = lax.dynamic_index_in_dim(vert_list, slot_index, axis=1, keepdims=False)
        k_far = lax.dynamic_index_in_dim(vert_k, slot_index, axis=1, keepdims=False)
        v_far = lax.dynamic_index_in_dim(vert_v, slot_index, axis=1, keepdims=False)
        hits = (offset_list[None, :, :] >= 1) & (
            query_blocks[:, None, None] - offset_list[None, :, :] == block_now[None, :, None]
        )
        allowed = (
            (block_now[None, :] >= 0)
            & (block_now[None, :] < query_blocks[:, None])
            & jnp.logical_not(jnp.any(hits, axis=2))
        )
        slot_scores = (
            jnp.einsum("nqhd,hkd->nqhk", q_tiles, k_far, preferred_element_type=jnp.float32)
            * score_scale
        )

        def weigh_far(prob_low):
            return jnp.einsum("nqhk,hkd->nqhd", prob_low, v_far, preferred_element_type=jnp.float32)

        return add_slot(running, slot_scores, allowed[:, None, :, None], weigh_far)

    vert_turns = jnp.max(jnp.sum((vert_list >= 0).astype(jnp.int32), axis=1))
    best, total, accum = lax.fori_loop(0, vert_turns, vert_slot, running)
    mixed = (
        (accum / total[..., None]).astype(jnp.bfloat16).reshape(seg_rows, per_device * HEAD_SIZE)
    )
    returned = lax.all_to_all(mixed, "uly", split_axis=0, concat_axis=1, tiled=True)
    return returned


MESH = pl.DeviceIdType.MESH
LOG2_E = 1.4426950408889634
HALVES = 2
PHASES = ((1, 0), (0, 0), (1, 1), (0, 1))
UP, DOWN, ACROSS, BESIDE, UP_TOO, DOWN_TOO, BESIDE_TOO = range(7)
SHORT = ()
GANG = 2


def axis_pair(half):
    return ("y", "x") if half == 0 else ("x", "y")


def whereabouts(group, member):
    return {"x": group // 2, "core": group % 2, "y": member % 2, "z": member // 2}


def flipped(where, axis):
    return {**where, axis: 1 - where[axis]}


def place_of(half, where, length):
    shared, other = axis_pair(half)
    return ((where["core"] * length + where["z"]) * 2 + where[other]) * 2 + where[shared]


def attend(units, k_buf, v_buf, table_ref, bias_ref):
    slots = range(table_ref.shape[1])
    rate = HEAD_SIZE ** (-0.5) * LOG2_E
    causal = lax.broadcasted_iota(
        jnp.int32, (BLOCK_TOKENS, BLOCK_TOKENS), 0
    ) >= lax.broadcasted_iota(jnp.int32, (BLOCK_TOKENS, BLOCK_TOKENS), 1)
    scores, probs, totals = [], [], []
    for q_ref, _, columns, line in units:
        keys = jnp.concatenate([k_buf[table_ref[line, slot]] for slot in slots], axis=0)
        scores.append(
            lax.dot_general(
                q_ref[:, columns],
                keys,
                (((1,), (1,)), ((), ())),
                preferred_element_type=jnp.float32,
            )
        )
    for score, (_, _, _, line) in zip(scores, units):
        pieces = []
        for slot in slots:
            piece = score[:, slot * BLOCK_TOKENS : (slot + 1) * BLOCK_TOKENS]
            if slot == 0:
                pieces.append(jnp.where(causal, piece, neg_large))
            else:
                pieces.append(piece + bias_ref[line, slot])
        best = functools.reduce(jnp.maximum, pieces)
        best = jnp.max(best, axis=1, keepdims=True)
        weights = [jnp.exp2((piece - best) * rate) for piece in pieces]
        total = functools.reduce(jnp.add, weights)
        totals.append(jnp.sum(total, axis=1, keepdims=True))
        probs.append(jnp.concatenate([weight.astype(jnp.bfloat16) for weight in weights], axis=1))
    for (_, o_ref, columns, line), prob, total in zip(units, probs, totals):
        values = jnp.concatenate([v_buf[table_ref[line, slot]] for slot in slots], axis=0)
        mixed = jnp.dot(prob, values, preferred_element_type=jnp.float32)
        o_ref[:, columns] = (mixed / total).astype(o_ref.dtype)


def split_kernel(
    uly_count,
    vert_hbm,
    slash_hbm,
    q_hbm,
    k_hbm,
    v_hbm,
    out_ref,
    vert_ref,
    slash_ref,
    list_sem,
    table_ref,
    bias_ref,
    k_own,
    v_own,
    load_sem,
    own_sem,
    ex_send,
    ex_recv,
    q_sem,
    q_send,
    q_recv,
    g_send,
    g_recv,
    b_recv,
    o_sem,
    o_send,
    o_recv,
    *buffers,
):
    length = uly_count // 2
    group, member = lax.axis_index("grp"), lax.axis_index("uly")
    me = whereabouts(group, member)
    z = me["z"]
    per_kv = q_hbm.shape[1] // KEY_VALUE_HEADS
    turns = per_kv // HEAD_SIZE
    gangs = turns // GANG
    held = buffers[:8]
    q_bufs = [buffers[8 + 2 * n : 10 + 2 * n] for n in range(4)]
    o_bufs = [buffers[16 + 2 * n : 18 + 2 * n] for n in range(4)]
    sources = (k_own, v_own)

    def block_at(where):
        return (where["x"] * 2 + where["core"]) * uly_count + where["z"] * 2 + where["y"]

    def device_at(where):
        return (where["x"] * 2 + where["core"], where["z"] * 2 + where["y"])

    def partner(half):
        return flipped(me, axis_pair(half)[0])

    def kv_head(half, n, where):
        return (half * 2 + where[axis_pair(half)[0]]) * 2 + n

    def lanes(start, width):
        return pl.ds(pl.multiple_of(start, HEAD_SIZE), width)

    lists = []
    for n, (source, target) in enumerate(((vert_hbm, vert_ref), (slash_hbm, slash_ref))):
        lists.append(pltpu.make_async_copy(source, target, list_sem.at[n]))
        lists[-1].start()
    loads = []
    for n, (source, target) in enumerate(((k_hbm, k_own), (v_hbm, v_own))):
        loads.append(pltpu.make_async_copy(source, target, load_sem.at[n]))
        loads[-1].start()
    own, q_own = {}, {}
    for half, n in PHASES:
        for kind, source in enumerate((k_hbm, v_hbm)):
            item = (half * 2 + n) * 2 + kind
            columns = lanes(kv_head(half, n, me) * HEAD_SIZE, HEAD_SIZE)
            own[item] = pltpu.make_async_copy(
                source.at[:, columns], held[item].at[place_of(half, me, length)], own_sem.at[item]
            )
            own[item].start()
    for half, n in PHASES:
        columns = lanes(kv_head(half, n, me) * per_kv, per_kv)
        q_own[half, n] = pltpu.make_async_copy(
            q_hbm.at[:, columns], q_bufs[half * 2 + n][0], q_sem.at[half * 2 + n]
        )
        q_own[half, n].start()

    barrier = pltpu.get_barrier_semaphore()
    around = [flipped(me, axis) for axis in ("x", "y", "core")]
    for where in around:
        pl.semaphore_signal(barrier, inc=1, device_id=device_at(where), device_id_type=MESH)

    def greet(step):
        pl.semaphore_signal(
            barrier, inc=1, device_id=device_at({**me, "z": z + step}), device_id_type=MESH
        )

    pl.when(z > 0)(lambda: greet(-1))
    pl.when(z < length - 1)(lambda: greet(1))
    count = len(around) + jnp.where(z > 0, 1, 0) + jnp.where(z < length - 1, 1, 0)
    pl.semaphore_wait(barrier, count)
    for load in loads:
        load.wait()

    def remote(source, target, send, recv, where):
        return pltpu.make_async_remote_copy(
            src_ref=source,
            dst_ref=target,
            send_sem=send,
            recv_sem=recv,
            device_id=device_at(where),
            device_id_type=MESH,
        )

    sent = []

    def begin(copy):
        copy.start()
        sent.append(copy)
        return copy

    exchanged, asked, answered, own_out = {}, {}, [], []

    def exchange(half, n):
        peer = partner(half)
        columns = lanes(kv_head(half, n, peer) * HEAD_SIZE, HEAD_SIZE)
        for kind in range(2):
            item = (half * 2 + n) * 2 + kind
            exchanged[item] = begin(
                remote(
                    sources[kind].at[:, columns],
                    held[item].at[place_of(half, me, length)],
                    ex_send.at[item],
                    ex_recv.at[item],
                    peer,
                )
            )

    def ask(half, n):
        peer = partner(half)
        columns = lanes(kv_head(half, n, peer) * per_kv, per_kv)
        asked[half, n] = begin(
            remote(
                q_hbm.at[:, columns],
                q_bufs[half * 2 + n][1],
                q_send.at[half * 2 + n],
                q_recv.at[half * 2 + n],
                peer,
            )
        )

    def part_of(item, core, slab, lane):
        other = axis_pair(item // 4)[1]
        side = me[other] if lane == 0 else 1 - me[other]
        return held[item].at[pl.ds(((core * length + slab) * 2 + side) * 2, 2)]

    def hop(item, slab, way, part=None):
        other = axis_pair(item // 4)[1]
        lane = 1 if way in (UP_TOO, DOWN_TOO, BESIDE_TOO) else 0
        if part is None:
            part = part_of(item, me["core"], slab, lane)
        if way in (BESIDE, BESIDE_TOO):
            where, recv = flipped(me, "core"), b_recv.at[item, slab, lane]
        elif way == ACROSS:
            where, recv = flipped(me, other), g_recv.at[item, slab, 1]
        else:
            where = {**me, "z": z + (1 if way in (UP, UP_TOO) else -1)}
            recv = g_recv.at[item, slab, lane]
        return remote(part, part, g_send.at[item, slab, way], recv, where)

    def wait_for(item, slab, lane):
        part = part_of(item, me["core"], slab, lane)
        recv = g_recv.at[item, slab, lane]
        remote(part, part, g_send.at[item, slab, 0], recv, me).wait_recv()

    def wait_beside(item, slab, lane):
        part = part_of(item, 1 - me["core"], slab, lane)
        recv = b_recv.at[item, slab, lane]
        remote(part, part, g_send.at[item, slab, 0], recv, me).wait_recv()

    def each_way(item, slab, ways, act, part=None):
        for way in ways:
            if way in (UP, UP_TOO):
                ok = z < length - 1
            elif way in (DOWN, DOWN_TOO):
                ok = z > 0
            elif way == ACROSS and item < 4:
                ok = me["x"] == 0
            else:
                ok = None
            if ok is None:
                act(hop(item, slab, way, part))
            else:
                pl.when(ok)(lambda way=way: act(hop(item, slab, way, part)))

    def started(copy):
        copy.start()

    def finished(copy):
        copy.wait_send()

    def visit(item, distance, act, wait=False):
        if distance == 0:
            each_way(item, z, (UP, DOWN, ACROSS, BESIDE), act)
            return
        across = () if item in SHORT and distance == 1 else (ACROSS,)

        @pl.when(z >= distance)
        def _():
            if wait:
                wait_for(item, z - distance, 0)
            each_way(item, z - distance, (UP,) + across + (BESIDE,), act)

        @pl.when(z + distance < length)
        def _():
            if wait:
                wait_for(item, z + distance, 0)
            each_way(item, z + distance, (DOWN,) + across + (BESIDE,), act)

    def visit_too(item, distance, act, wait=False):
        ways = (UP_TOO, DOWN_TOO, BESIDE_TOO) if distance == 0 and item in SHORT else (BESIDE_TOO,)

        @crossed(item)
        def _():
            @pl.when(z >= distance)
            def _():
                if wait:
                    wait_for(item, z - distance, 1)
                each_way(item, z - distance, ways, act)

            if distance:
                @pl.when(z + distance < length)
                def _():
                    if wait:
                        wait_for(item, z + distance, 1)
                    each_way(item, z + distance, ways, act)

    def crossed(item):
        return lambda body: body() if item >= 4 else pl.when(me["x"] == 1)(body)

    def items_of(phase):
        half, n = PHASES[phase]
        return [(half * 2 + n) * 2 + kind for kind in range(2)]

    def launch(item):
        own[item].wait()
        exchanged[item].wait_recv()
        visit(item, 0, started)

    def launch_early(item, mine):
        half = item // 4
        where = me if mine else partner(half)
        if mine:
            own[item].wait()
        else:
            exchanged[item].wait_recv()
        block = held[item].at[pl.ds(place_of(half, where, length), 1)]
        each_way(item, z, (UP, DOWN, ACROSS, BESIDE), started, block)

    def step(item, distance):
        if distance == 0:
            launch(item)
        elif distance < 0:
            visit_too(item, -1 - distance, started, wait=True)
        else:
            visit(item, distance, started, wait=True)

    def steps(phase, distance):
        todo = [(item, distance) for item in items_of(phase)]
        short = [item for item in items_of(phase) if item in SHORT]
        if distance == 1:
            todo += [(item, -1) for item in short]
        if distance == length - 1:
            todo += [(item, -2) for item in short]
        return todo

    def settle(phase):
        for item in items_of(phase):
            for distance in range(2 if item in SHORT else 0, length):
                visit_too(item, distance, started, wait=True)
        for item in items_of(phase):
            for slab in range(length):
                wait_beside(item, slab, 0)

            @crossed(item)
            def _():
                for slab in range(length):
                    wait_beside(item, slab, 1)

        q_own[PHASES[phase]].wait()
        asked[PHASES[phase]].wait_recv()

    def drain(item):
        for distance in range(length):
            visit(item, distance, finished)
            visit_too(item, distance, finished)

    def answer(phase, gang):
        half, n = PHASES[phase]
        index = half * 2 + n
        width = GANG * HEAD_SIZE
        columns = lanes(kv_head(half, n, me) * per_kv + gang * width, width)
        local = pl.ds(gang * width, width)
        copy = begin(
            remote(
                o_bufs[index][1].at[:, local],
                out_ref.at[:, columns],
                o_send.at[index, gang],
                o_recv.at[index, gang],
                partner(half),
            )
        )
        answered.append(copy)
        copy = pltpu.make_async_copy(
            o_bufs[index][0].at[:, local], out_ref.at[:, columns], o_sem.at[index, gang]
        )
        copy.start()
        own_out.append(copy)

    def compute(phase, gang):
        half, n = PHASES[phase]
        index = half * 2 + n
        units = []
        for turn in range(gang * GANG, (gang + 1) * GANG):
            for side in range(2):
                units.append(
                    (
                        q_bufs[index][side],
                        o_bufs[index][side],
                        pl.ds(turn * HEAD_SIZE, HEAD_SIZE),
                        (phase * turns + turn) * 2 + side,
                    )
                )
        k_item, v_item = items_of(phase)
        attend(units, held[k_item], held[v_item], table_ref, bias_ref)

    def tabulate(phase):
        half, n = PHASES[phase]
        first = kv_head(half, n, me) * turns
        if phase == 0:
            for copy in lists:
                copy.wait()

        def place_at(block):
            group, member = lax.div(block, uly_count), lax.rem(block, uly_count)
            where = {
                "x": lax.div(group, 2),
                "core": lax.rem(group, 2),
                "y": lax.rem(member, 2),
                "z": lax.div(member, 2),
            }
            return place_of(half, where, length)

        @pl.loop(0, turns)
        def _(turn):
            q_head = first + turn
            offsets = [slash_ref[slot, q_head] for slot in range(slash_ref.shape[0])]
            listed = [vert_ref[slot, q_head] for slot in range(vert_ref.shape[0])]
            for side, where in enumerate((me, partner(half))):
                line = (phase * turns + turn) * 2 + side
                here = block_at(where)
                rows = [(here, None)]
                targets = []
                for offset in offsets:
                    ok = (offset >= 1) & (here - offset >= 0)
                    targets.append(jnp.where(ok, here - offset, -1))
                    rows.append((here - offset, ok))
                for block in listed:
                    ok = (block >= 0) & (block < here)
                    for target in targets:
                        ok = ok & (block != target)
                    rows.append((block, ok))
                for slot, (block, ok) in enumerate(rows):
                    if ok is None:
                        table_ref[line, slot] = place_at(block)
                    else:
                        table_ref[line, slot] = place_at(jnp.where(ok, block, here))
                        bias_ref[line, slot] = jnp.where(ok, 0.0, neg_large).astype(jnp.float32)

    def run(todo):
        for item, distance in todo:
            step(item, distance)

    for phase in range(4):
        exchange(*PHASES[phase])
    ask(*PHASES[0])
    for mine in (True, False):
        for item in items_of(0):
            launch_early(item, mine)
    tabulate(0)
    run(steps(0, 1) + steps(1, 0))
    tabulate(1)
    run(steps(0, 2))
    tabulate(2)
    run(steps(1, 1) + steps(0, 3))
    ask(*PHASES[1])
    ask(*PHASES[3])
    tabulate(3)
    run(steps(2, 0) + steps(1, 2) + steps(2, 1) + steps(1, 3))
    ask(*PHASES[2])
    run(steps(3, 0))
    between = (
        ((), (), steps(2, 2)[:1], steps(2, 2)[1:]),
        (steps(3, 1)[:1], steps(3, 1)[1:], steps(2, 3)[:1], steps(2, 3)[1:] + steps(3, 2)),
        (steps(3, 3)[:1], steps(3, 3)[1:], (), ()),
        ((), (), (), ()),
    )
    held_back = {0: (0,), 1: (1,), 2: (2,)}
    for phase in range(4):
        settle(phase)
        for gang in range(gangs):
            compute(phase, gang)
            run(between[phase][gang])
            if phase == 3:
                answer(phase, gang)
        for ready in held_back.get(phase, ()):
            for gang in range(gangs):
                answer(ready, gang)
    for copy in sent:
        copy.wait_send()
    for item in range(8):
        drain(item)
    for copy in answered:
        copy.wait_recv()
    for copy in own_out:
        copy.wait()


def split_shards(queries, key_state_rows, value_state_rows, vert_blocks, slash_offsets):
    group_count, uly_count = lax.axis_size("grp"), lax.axis_size("uly")
    blocks = group_count * uly_count
    length = uly_count // 2
    turns = QUERY_HEADS // KEY_VALUE_HEADS
    slots = 1 + slash_offsets.shape[1] + vert_blocks.shape[1]
    dtype = queries.dtype
    hbm = pl.BlockSpec(memory_space=pl.ANY)
    dma = pltpu.SemaphoreType.DMA
    share = (BLOCK_TOKENS, turns * HEAD_SIZE)
    return pl.pallas_call(
        functools.partial(split_kernel, uly_count),
        out_shape=pltpu.VMEM(queries.shape, dtype),
        in_specs=[hbm] * 5,
        out_specs=pl.BlockSpec(memory_space=pltpu.VMEM),
        scratch_shapes=[
            pltpu.SMEM(vert_blocks.shape[::-1], jnp.int32),
            pltpu.SMEM(slash_offsets.shape[::-1], jnp.int32),
            dma((2,)),
            pltpu.SMEM((8 * turns, slots), jnp.int32),
            pltpu.SMEM((8 * turns, slots), jnp.float32),
            pltpu.VMEM(key_state_rows.shape, dtype),
            pltpu.VMEM(value_state_rows.shape, dtype),
            dma((2,)),
            dma((8,)),
            dma((8,)),
            dma((8,)),
            dma((4,)),
            dma((4,)),
            dma((4,)),
            dma((8, length, 7)),
            dma((8, length, 2)),
            dma((8, length, 2)),
            dma((4, turns // GANG)),
            dma((4, turns // GANG)),
            dma((4, turns // GANG)),
        ]
        + [pltpu.VMEM((blocks, BLOCK_TOKENS, HEAD_SIZE), dtype)] * 8
        + [pltpu.VMEM(share, dtype)] * 16,
        compiler_params=pltpu.CompilerParams(collective_id=0, has_side_effects=True),
        name="split_and_attend",
    )(
        vert_blocks.T,
        slash_offsets.T,
        queries,
        key_state_rows,
        value_state_rows,
    )


def chosen(queries, key_state_rows, *rest):
    group_count, uly_count = lax.axis_size("grp"), lax.axis_size("uly")
    fits = (
        group_count == 4
        and uly_count == 8
        and KEY_VALUE_HEADS == 4 * HALVES
        and queries.shape[0] == BLOCK_TOKENS
    )
    plan = split_shards if fits else shards
    return plan(queries, key_state_rows, *rest)


def solution(mesh):
    return jax.shard_map(
        chosen,
        mesh=mesh,
        in_specs=(
            P(("grp", "uly"), None),
            P(("grp", "uly"), None),
            P(("grp", "uly"), None),
            P(),
            P(),
        ),
        out_specs=P(("grp", "uly"), None),
        check_vma=False,
    )
```

```python
import functools

import jax
import jax.numpy as jnp
import numpy as np
from jax import lax
from jax.experimental import pallas as pl
from jax.experimental.pallas import tpu as pltpu
from jax.sharding import PartitionSpec as P

QUERY_HEADS = 64
KEY_VALUE_HEADS = 8
HEAD_SIZE = 128
BLOCK_TOKENS = 128


neg_large = -1e30


def passed_along(value, axis, steps):
    count = lax.axis_size(axis)
    initial, last = (max(0, -steps), min(count, count - steps))
    return lax.ppermute(value, axis, [(source, source + steps) for source in range(initial, last)])


def add_slot(running, slot_scores, allowed, weigh):
    best, total, accum = running
    slot_scores = jnp.where(allowed, slot_scores, neg_large)
    new_best = jnp.maximum(best, jnp.max(slot_scores, axis=-1))
    factor = jnp.exp(best - new_best)
    weights = jnp.where(allowed, jnp.exp(slot_scores - new_best[..., None]), 0.0)
    total = total * factor + jnp.sum(weights, axis=-1)
    accum = accum * factor[..., None] + weigh(weights.astype(jnp.bfloat16))
    return (new_best, total, accum)


def shards(queries, key_state_rows, value_state_rows, vert_blocks, slash_offsets):
    ulysses_count = lax.axis_size("uly")
    group_id = lax.axis_index("grp")
    uly_id = lax.axis_index("uly")
    per_device = QUERY_HEADS // ulysses_count
    group_width = QUERY_HEADS // KEY_VALUE_HEADS
    token_rows = queries.shape[0]
    ordering = jnp.arange(QUERY_HEADS, dtype=jnp.int32)
    heads_per_slot = np.arange(ulysses_count) * per_device // group_width
    key_outgoing = key_state_rows.reshape(token_rows, KEY_VALUE_HEADS, HEAD_SIZE)[
        :, heads_per_slot
    ].reshape(token_rows, ulysses_count * HEAD_SIZE)
    value_outgoing = value_state_rows.reshape(token_rows, KEY_VALUE_HEADS, HEAD_SIZE)[
        :, heads_per_slot
    ].reshape(token_rows, ulysses_count * HEAD_SIZE)
    q_group, k_group, v_group = (
        lax.all_to_all(queries, "uly", split_axis=1, concat_axis=0, tiled=True),
        lax.all_to_all(key_outgoing, "uly", split_axis=1, concat_axis=0, tiled=True),
        lax.all_to_all(value_outgoing, "uly", split_axis=1, concat_axis=0, tiled=True),
    )
    seg_rows = q_group.shape[0]
    block_count = seg_rows // BLOCK_TOKENS
    reach = block_count // 2
    q_tiles = q_group.reshape(block_count, BLOCK_TOKENS, per_device, HEAD_SIZE)
    key_block_tiles = k_group.reshape(block_count, BLOCK_TOKENS, HEAD_SIZE)
    value_block_tiles = v_group.reshape(block_count, BLOCK_TOKENS, HEAD_SIZE)
    prior_k, prior_v = passed_along(
        (key_block_tiles[block_count - reach :], value_block_tiles[block_count - reach :]), "grp", 1
    )
    k_wide = jnp.concatenate([prior_k, key_block_tiles], axis=0)
    v_wide = jnp.concatenate([prior_v, value_block_tiles], axis=0)
    heads_here = lax.dynamic_slice_in_dim(ordering, uly_id * per_device, per_device)
    vert_list = jnp.take(vert_blocks, heads_here, axis=0)
    offset_list = jnp.take(slash_offsets, heads_here, axis=0)
    local_block = jnp.where(vert_list >= 0, vert_list % block_count, 0)
    owned = (vert_list >= 0) & (vert_list // block_count == group_id)
    pick_k = jnp.where(
        owned[:, :, None, None], key_block_tiles[local_block], jnp.zeros((), jnp.bfloat16)
    )
    pick_v = jnp.where(
        owned[:, :, None, None], value_block_tiles[local_block], jnp.zeros((), jnp.bfloat16)
    )
    summed_k, summed_v = (
        lax.psum(pick_k.astype(jnp.float32).astype(jnp.bfloat16), "grp").astype(jnp.float32),
        lax.psum(pick_v.astype(jnp.float32).astype(jnp.bfloat16), "grp").astype(jnp.float32),
    )
    vert_k = summed_k.astype(jnp.bfloat16)
    vert_v = summed_v.astype(jnp.bfloat16)
    query_blocks = group_id * block_count + jnp.arange(block_count, dtype=jnp.int32)
    score_scale = HEAD_SIZE ** (-0.5)
    causal = (jnp.arange(BLOCK_TOKENS)[:, None] >= jnp.arange(BLOCK_TOKENS)[None, :])[
        None, :, None, :
    ]
    diag_scores = (
        jnp.einsum("nqhd,nkd->nqhk", q_tiles, key_block_tiles, preferred_element_type=jnp.float32)
        * score_scale
    )
    diag_scores = jnp.where(causal, diag_scores, neg_large)
    best = jnp.max(diag_scores, axis=-1)
    diag_weights = jnp.where(causal, jnp.exp(diag_scores - best[..., None]), 0.0)
    total = jnp.sum(diag_weights, axis=-1)
    accum = jnp.einsum(
        "nqhk,nkd->nqhd",
        diag_weights.astype(jnp.bfloat16),
        value_block_tiles,
        preferred_element_type=jnp.float32,
    )
    running = (best, total, accum)

    def slash_slot(slot_index, running):
        offset_now = lax.dynamic_index_in_dim(offset_list, slot_index, axis=1, keepdims=False)
        starts = jnp.where(offset_now >= 1, reach - offset_now, 0)

        def near_slice(begin_at):
            return (
                lax.dynamic_slice_in_dim(k_wide, begin_at, block_count, 0),
                lax.dynamic_slice_in_dim(v_wide, begin_at, block_count, 0),
            )

        k_near, v_near = jax.vmap(near_slice)(starts)
        allowed = (offset_now[None, :] >= 1) & (query_blocks[:, None] - offset_now[None, :] >= 0)
        slot_scores = (
            jnp.einsum("nqhd,hnkd->nqhk", q_tiles, k_near, preferred_element_type=jnp.float32)
            * score_scale
        )

        def weigh_near(prob_low):
            return jnp.einsum(
                "nqhk,hnkd->nqhd", prob_low, v_near, preferred_element_type=jnp.float32
            )

        return add_slot(running, slot_scores, allowed[:, None, :, None], weigh_near)

    slash_turns = jnp.max(jnp.sum((offset_list >= 1).astype(jnp.int32), axis=1))
    running = lax.fori_loop(0, slash_turns, slash_slot, running)

    def vert_slot(slot_index, running):
        block_now = lax.dynamic_index_in_dim(vert_list, slot_index, axis=1, keepdims=False)
        k_far = lax.dynamic_index_in_dim(vert_k, slot_index, axis=1, keepdims=False)
        v_far = lax.dynamic_index_in_dim(vert_v, slot_index, axis=1, keepdims=False)
        hits = (offset_list[None, :, :] >= 1) & (
            query_blocks[:, None, None] - offset_list[None, :, :] == block_now[None, :, None]
        )
        allowed = (
            (block_now[None, :] >= 0)
            & (block_now[None, :] < query_blocks[:, None])
            & jnp.logical_not(jnp.any(hits, axis=2))
        )
        slot_scores = (
            jnp.einsum("nqhd,hkd->nqhk", q_tiles, k_far, preferred_element_type=jnp.float32)
            * score_scale
        )

        def weigh_far(prob_low):
            return jnp.einsum("nqhk,hkd->nqhd", prob_low, v_far, preferred_element_type=jnp.float32)

        return add_slot(running, slot_scores, allowed[:, None, :, None], weigh_far)

    vert_turns = jnp.max(jnp.sum((vert_list >= 0).astype(jnp.int32), axis=1))
    best, total, accum = lax.fori_loop(0, vert_turns, vert_slot, running)
    mixed = (
        (accum / total[..., None]).astype(jnp.bfloat16).reshape(seg_rows, per_device * HEAD_SIZE)
    )
    returned = lax.all_to_all(mixed, "uly", split_axis=0, concat_axis=1, tiled=True)
    return returned


MESH = pl.DeviceIdType.MESH
LOG2_E = 1.4426950408889634
HALVES = 2
PHASES = ((1, 0), (0, 0), (1, 1), (0, 1))
UP, DOWN, ACROSS, BESIDE, UP_TOO, DOWN_TOO, BESIDE_TOO = range(7)
SHORT = ()
GANG = 2


def axis_pair(half):
    return ("y", "x") if half == 0 else ("x", "y")


def whereabouts(group, member):
    return {"x": group // 2, "core": group % 2, "y": member % 2, "z": member // 2}


def flipped(where, axis):
    return {**where, axis: 1 - where[axis]}


def place_of(half, where, length):
    shared, other = axis_pair(half)
    return ((where["core"] * length + where["z"]) * 2 + where[other]) * 2 + where[shared]


def attend(units, k_buf, v_buf, table_ref, bias_ref):
    slots = range(table_ref.shape[1])
    rate = HEAD_SIZE ** (-0.5) * LOG2_E
    causal = lax.broadcasted_iota(
        jnp.int32, (BLOCK_TOKENS, BLOCK_TOKENS), 0
    ) >= lax.broadcasted_iota(jnp.int32, (BLOCK_TOKENS, BLOCK_TOKENS), 1)
    scores, probs, totals = [], [], []
    for q_ref, _, columns, line in units:
        keys = jnp.concatenate([k_buf[table_ref[line, slot]] for slot in slots], axis=0)
        scores.append(
            lax.dot_general(
                q_ref[:, columns],
                keys,
                (((1,), (1,)), ((), ())),
                preferred_element_type=jnp.float32,
            )
        )
    for score, (_, _, _, line) in zip(scores, units):
        pieces = []
        for slot in slots:
            piece = score[:, slot * BLOCK_TOKENS : (slot + 1) * BLOCK_TOKENS]
            if slot == 0:
                pieces.append(jnp.where(causal, piece, neg_large))
            else:
                pieces.append(piece + bias_ref[line, slot])
        best = functools.reduce(jnp.maximum, pieces)
        best = jnp.max(best, axis=1, keepdims=True)
        weights = [jnp.exp2((piece - best) * rate) for piece in pieces]
        total = functools.reduce(jnp.add, weights)
        totals.append(jnp.sum(total, axis=1, keepdims=True))
        probs.append(jnp.concatenate([weight.astype(jnp.bfloat16) for weight in weights], axis=1))
    for (_, o_ref, columns, line), prob, total in zip(units, probs, totals):
        values = jnp.concatenate([v_buf[table_ref[line, slot]] for slot in slots], axis=0)
        mixed = jnp.dot(prob, values, preferred_element_type=jnp.float32)
        o_ref[:, columns] = (mixed / total).astype(o_ref.dtype)


def split_kernel(
    uly_count,
    vert_hbm,
    slash_hbm,
    q_hbm,
    k_hbm,
    v_hbm,
    out_ref,
    vert_ref,
    slash_ref,
    list_sem,
    table_ref,
    bias_ref,
    k_own,
    v_own,
    load_sem,
    own_sem,
    ex_send,
    ex_recv,
    q_sem,
    q_send,
    q_recv,
    g_send,
    g_recv,
    b_recv,
    o_sem,
    o_send,
    o_recv,
    *buffers,
):
    length = uly_count // 2
    group, member = lax.axis_index("grp"), lax.axis_index("uly")
    me = whereabouts(group, member)
    z = me["z"]
    per_kv = q_hbm.shape[1] // KEY_VALUE_HEADS
    turns = per_kv // HEAD_SIZE
    gangs = turns // GANG
    held = buffers[:8]
    q_bufs = [buffers[8 + 2 * n : 10 + 2 * n] for n in range(4)]
    o_bufs = [buffers[16 + 2 * n : 18 + 2 * n] for n in range(4)]
    sources = (k_own, v_own)

    def block_at(where):
        return (where["x"] * 2 + where["core"]) * uly_count + where["z"] * 2 + where["y"]

    def device_at(where):
        return (where["x"] * 2 + where["core"], where["z"] * 2 + where["y"])

    def partner(half):
        return flipped(me, axis_pair(half)[0])

    def kv_head(half, n, where):
        return (half * 2 + where[axis_pair(half)[0]]) * 2 + n

    def lanes(start, width):
        return pl.ds(pl.multiple_of(start, HEAD_SIZE), width)

    lists = []
    for n, (source, target) in enumerate(((vert_hbm, vert_ref), (slash_hbm, slash_ref))):
        lists.append(pltpu.make_async_copy(source, target, list_sem.at[n]))
        lists[-1].start()
    loads = []
    for n, (source, target) in enumerate(((k_hbm, k_own), (v_hbm, v_own))):
        loads.append(pltpu.make_async_copy(source, target, load_sem.at[n]))
        loads[-1].start()
    own, q_own = {}, {}
    for half, n in PHASES:
        for kind, source in enumerate((k_hbm, v_hbm)):
            item = (half * 2 + n) * 2 + kind
            columns = lanes(kv_head(half, n, me) * HEAD_SIZE, HEAD_SIZE)
            own[item] = pltpu.make_async_copy(
                source.at[:, columns], held[item].at[place_of(half, me, length)], own_sem.at[item]
            )
            own[item].start()
    for half, n in PHASES:
        columns = lanes(kv_head(half, n, me) * per_kv, per_kv)
        q_own[half, n] = pltpu.make_async_copy(
            q_hbm.at[:, columns], q_bufs[half * 2 + n][0], q_sem.at[half * 2 + n]
        )
        q_own[half, n].start()

    barrier = pltpu.get_barrier_semaphore()
    around = [flipped(me, axis) for axis in ("x", "y", "core")]
    for where in around:
        pl.semaphore_signal(barrier, inc=1, device_id=device_at(where), device_id_type=MESH)

    def greet(step):
        pl.semaphore_signal(
            barrier, inc=1, device_id=device_at({**me, "z": z + step}), device_id_type=MESH
        )

    pl.when(z > 0)(lambda: greet(-1))
    pl.when(z < length - 1)(lambda: greet(1))
    count = len(around) + jnp.where(z > 0, 1, 0) + jnp.where(z < length - 1, 1, 0)
    pl.semaphore_wait(barrier, count)
    for load in loads:
        load.wait()

    def remote(source, target, send, recv, where):
        return pltpu.make_async_remote_copy(
            src_ref=source,
            dst_ref=target,
            send_sem=send,
            recv_sem=recv,
            device_id=device_at(where),
            device_id_type=MESH,
        )

    sent = []

    def begin(copy):
        copy.start()
        sent.append(copy)
        return copy

    exchanged, asked, answered, own_out = {}, {}, [], []

    def exchange(half, n):
        peer = partner(half)
        columns = lanes(kv_head(half, n, peer) * HEAD_SIZE, HEAD_SIZE)
        for kind in range(2):
            item = (half * 2 + n) * 2 + kind
            exchanged[item] = begin(
                remote(
                    sources[kind].at[:, columns],
                    held[item].at[place_of(half, me, length)],
                    ex_send.at[item],
                    ex_recv.at[item],
                    peer,
                )
            )

    def ask(half, n):
        peer = partner(half)
        columns = lanes(kv_head(half, n, peer) * per_kv, per_kv)
        asked[half, n] = begin(
            remote(
                q_hbm.at[:, columns],
                q_bufs[half * 2 + n][1],
                q_send.at[half * 2 + n],
                q_recv.at[half * 2 + n],
                peer,
            )
        )

    def part_of(item, core, slab, lane):
        other = axis_pair(item // 4)[1]
        side = me[other] if lane == 0 else 1 - me[other]
        return held[item].at[pl.ds(((core * length + slab) * 2 + side) * 2, 2)]

    def hop(item, slab, way, part=None):
        other = axis_pair(item // 4)[1]
        lane = 1 if way in (UP_TOO, DOWN_TOO, BESIDE_TOO) else 0
        if part is None:
            part = part_of(item, me["core"], slab, lane)
        if way in (BESIDE, BESIDE_TOO):
            where, recv = flipped(me, "core"), b_recv.at[item, slab, lane]
        elif way == ACROSS:
            where, recv = flipped(me, other), g_recv.at[item, slab, 1]
        else:
            where = {**me, "z": z + (1 if way in (UP, UP_TOO) else -1)}
            recv = g_recv.at[item, slab, lane]
        return remote(part, part, g_send.at[item, slab, way], recv, where)

    def wait_for(item, slab, lane):
        part = part_of(item, me["core"], slab, lane)
        recv = g_recv.at[item, slab, lane]
        remote(part, part, g_send.at[item, slab, 0], recv, me).wait_recv()

    def wait_beside(item, slab, lane):
        part = part_of(item, 1 - me["core"], slab, lane)
        recv = b_recv.at[item, slab, lane]
        remote(part, part, g_send.at[item, slab, 0], recv, me).wait_recv()

    def each_way(item, slab, ways, act, part=None):
        for way in ways:
            if way in (UP, UP_TOO):
                ok = z < length - 1
            elif way in (DOWN, DOWN_TOO):
                ok = z > 0
            elif way == ACROSS and item < 4:
                ok = me["x"] == 0
            else:
                ok = None
            if ok is None:
                act(hop(item, slab, way, part))
            else:
                pl.when(ok)(lambda way=way: act(hop(item, slab, way, part)))

    def started(copy):
        copy.start()

    def finished(copy):
        copy.wait_send()

    def visit(item, distance, act, wait=False):
        if distance == 0:
            each_way(item, z, (UP, DOWN, ACROSS, BESIDE), act)
            return
        across = () if item in SHORT and distance == 1 else (ACROSS,)

        @pl.when(z >= distance)
        def _():
            if wait:
                wait_for(item, z - distance, 0)
            each_way(item, z - distance, (UP,) + across + (BESIDE,), act)

        @pl.when(z + distance < length)
        def _():
            if wait:
                wait_for(item, z + distance, 0)
            each_way(item, z + distance, (DOWN,) + across + (BESIDE,), act)

    def visit_too(item, distance, act, wait=False):
        ways = (UP_TOO, DOWN_TOO, BESIDE_TOO) if distance == 0 and item in SHORT else (BESIDE_TOO,)

        @crossed(item)
        def _():
            @pl.when(z >= distance)
            def _():
                if wait:
                    wait_for(item, z - distance, 1)
                each_way(item, z - distance, ways, act)

            if distance:
                @pl.when(z + distance < length)
                def _():
                    if wait:
                        wait_for(item, z + distance, 1)
                    each_way(item, z + distance, ways, act)

    def crossed(item):
        return lambda body: body() if item >= 4 else pl.when(me["x"] == 1)(body)

    def items_of(phase):
        half, n = PHASES[phase]
        return [(half * 2 + n) * 2 + kind for kind in range(2)]

    def launch(item):
        own[item].wait()
        exchanged[item].wait_recv()
        visit(item, 0, started)

    def launch_early(item, mine):
        half = item // 4
        where = me if mine else partner(half)
        if mine:
            own[item].wait()
        else:
            exchanged[item].wait_recv()
        block = held[item].at[pl.ds(place_of(half, where, length), 1)]
        each_way(item, z, (UP, DOWN, ACROSS, BESIDE), started, block)

    def step(item, distance):
        if distance == 0:
            launch(item)
        elif distance < 0:
            visit_too(item, -1 - distance, started, wait=True)
        else:
            visit(item, distance, started, wait=True)

    def steps(phase, distance):
        todo = [(item, distance) for item in items_of(phase)]
        short = [item for item in items_of(phase) if item in SHORT]
        if distance == 1:
            todo += [(item, -1) for item in short]
        if distance == length - 1:
            todo += [(item, -2) for item in short]
        return todo

    def settle(phase):
        for item in items_of(phase):
            for distance in range(2 if item in SHORT else 0, length):
                visit_too(item, distance, started, wait=True)
        for item in items_of(phase):
            for slab in range(length):
                wait_beside(item, slab, 0)

            @crossed(item)
            def _():
                for slab in range(length):
                    wait_beside(item, slab, 1)

        q_own[PHASES[phase]].wait()
        asked[PHASES[phase]].wait_recv()

    def drain(item):
        for distance in range(length):
            visit(item, distance, finished)
            visit_too(item, distance, finished)

    def answer(phase, gang):
        half, n = PHASES[phase]
        index = half * 2 + n
        width = GANG * HEAD_SIZE
        columns = lanes(kv_head(half, n, me) * per_kv + gang * width, width)
        local = pl.ds(gang * width, width)
        copy = begin(
            remote(
                o_bufs[index][1].at[:, local],
                out_ref.at[:, columns],
                o_send.at[index, gang],
                o_recv.at[index, gang],
                partner(half),
            )
        )
        answered.append(copy)
        copy = pltpu.make_async_copy(
            o_bufs[index][0].at[:, local], out_ref.at[:, columns], o_sem.at[index, gang]
        )
        copy.start()
        own_out.append(copy)

    def compute(phase, gang):
        half, n = PHASES[phase]
        index = half * 2 + n
        units = []
        for turn in range(gang * GANG, (gang + 1) * GANG):
            for side in range(2):
                units.append(
                    (
                        q_bufs[index][side],
                        o_bufs[index][side],
                        pl.ds(turn * HEAD_SIZE, HEAD_SIZE),
                        (phase * turns + turn) * 2 + side,
                    )
                )
        k_item, v_item = items_of(phase)
        attend(units, held[k_item], held[v_item], table_ref, bias_ref)

    def tabulate(phase):
        half, n = PHASES[phase]
        first = kv_head(half, n, me) * turns
        if phase == 0:
            for copy in lists:
                copy.wait()

        def place_at(block):
            group, member = lax.div(block, uly_count), lax.rem(block, uly_count)
            where = {
                "x": lax.div(group, 2),
                "core": lax.rem(group, 2),
                "y": lax.rem(member, 2),
                "z": lax.div(member, 2),
            }
            return place_of(half, where, length)

        @pl.loop(0, turns)
        def _(turn):
            q_head = first + turn
            offsets = [slash_ref[slot, q_head] for slot in range(slash_ref.shape[0])]
            listed = [vert_ref[slot, q_head] for slot in range(vert_ref.shape[0])]
            for side, where in enumerate((me, partner(half))):
                line = (phase * turns + turn) * 2 + side
                here = block_at(where)
                rows = [(here, None)]
                targets = []
                for offset in offsets:
                    ok = (offset >= 1) & (here - offset >= 0)
                    targets.append(jnp.where(ok, here - offset, -1))
                    rows.append((here - offset, ok))
                for block in listed:
                    ok = (block >= 0) & (block < here)
                    for target in targets:
                        ok = ok & (block != target)
                    rows.append((block, ok))
                for slot, (block, ok) in enumerate(rows):
                    if ok is None:
                        table_ref[line, slot] = place_at(block)
                    else:
                        table_ref[line, slot] = place_at(jnp.where(ok, block, here))
                        bias_ref[line, slot] = jnp.where(ok, 0.0, neg_large).astype(jnp.float32)

    def run(todo):
        for item, distance in todo:
            step(item, distance)

    for phase in range(4):
        exchange(*PHASES[phase])
    ask(*PHASES[0])
    for mine in (True, False):
        for item in items_of(0):
            launch_early(item, mine)
    tabulate(0)
    run(steps(0, 1) + steps(1, 0))
    tabulate(1)
    run(steps(0, 2))
    tabulate(2)
    run(steps(1, 1) + steps(0, 3))
    ask(*PHASES[1])
    ask(*PHASES[3])
    tabulate(3)
    run(steps(2, 0) + steps(1, 2) + steps(2, 1) + steps(1, 3))
    ask(*PHASES[2])
    run(steps(3, 0))
    between = (
        ((), steps(2, 2)[:1], steps(2, 2)[1:], ()),
        (steps(3, 1), steps(2, 3)[:1], steps(2, 3)[1:], steps(3, 2)),
        (steps(3, 3)[:1], steps(3, 3)[1:], (), ()),
        ((), (), (), ()),
    )
    held_back = {0: (0,), 1: (1,), 2: (2,)}
    for phase in range(4):
        settle(phase)
        for gang in range(gangs):
            compute(phase, gang)
            run(between[phase][gang])
            if phase == 3:
                answer(phase, gang)
        for ready in held_back.get(phase, ()):
            for gang in range(gangs):
                answer(ready, gang)
    for copy in sent:
        copy.wait_send()
    for item in range(8):
        drain(item)
    for copy in answered:
        copy.wait_recv()
    for copy in own_out:
        copy.wait()


def split_shards(queries, key_state_rows, value_state_rows, vert_blocks, slash_offsets):
    group_count, uly_count = lax.axis_size("grp"), lax.axis_size("uly")
    blocks = group_count * uly_count
    length = uly_count // 2
    turns = QUERY_HEADS // KEY_VALUE_HEADS
    slots = 1 + slash_offsets.shape[1] + vert_blocks.shape[1]
    dtype = queries.dtype
    hbm = pl.BlockSpec(memory_space=pl.ANY)
    dma = pltpu.SemaphoreType.DMA
    share = (BLOCK_TOKENS, turns * HEAD_SIZE)
    return pl.pallas_call(
        functools.partial(split_kernel, uly_count),
        out_shape=pltpu.VMEM(queries.shape, dtype),
        in_specs=[hbm] * 5,
        out_specs=pl.BlockSpec(memory_space=pltpu.VMEM),
        scratch_shapes=[
            pltpu.SMEM(vert_blocks.shape[::-1], jnp.int32),
            pltpu.SMEM(slash_offsets.shape[::-1], jnp.int32),
            dma((2,)),
            pltpu.SMEM((8 * turns, slots), jnp.int32),
            pltpu.SMEM((8 * turns, slots), jnp.float32),
            pltpu.VMEM(key_state_rows.shape, dtype),
            pltpu.VMEM(value_state_rows.shape, dtype),
            dma((2,)),
            dma((8,)),
            dma((8,)),
            dma((8,)),
            dma((4,)),
            dma((4,)),
            dma((4,)),
            dma((8, length, 7)),
            dma((8, length, 2)),
            dma((8, length, 2)),
            dma((4, turns // GANG)),
            dma((4, turns // GANG)),
            dma((4, turns // GANG)),
        ]
        + [pltpu.VMEM((blocks, BLOCK_TOKENS, HEAD_SIZE), dtype)] * 8
        + [pltpu.VMEM(share, dtype)] * 16,
        compiler_params=pltpu.CompilerParams(collective_id=0, has_side_effects=True),
        name="split_and_attend",
    )(
        vert_blocks.T,
        slash_offsets.T,
        queries,
        key_state_rows,
        value_state_rows,
    )


def chosen(queries, key_state_rows, *rest):
    group_count, uly_count = lax.axis_size("grp"), lax.axis_size("uly")
    fits = (
        group_count == 4
        and uly_count == 8
        and KEY_VALUE_HEADS == 4 * HALVES
        and queries.shape[0] == BLOCK_TOKENS
    )
    plan = split_shards if fits else shards
    return plan(queries, key_state_rows, *rest)


def solution(mesh):
    return jax.shard_map(
        chosen,
        mesh=mesh,
        in_specs=(
            P(("grp", "uly"), None),
            P(("grp", "uly"), None),
            P(("grp", "uly"), None),
            P(),
            P(),
        ),
        out_specs=P(("grp", "uly"), None),
        check_vma=False,
    )
```
